256 devices in a mesh: grp: 8 (over x, core), mem: 32 (over y, z).
Axes of the slice: x: 4, y: 4, z: 8, core: 2. Of those that a mesh axis runs over, the one named last changes fastest.
Arguments:
- features: bfloat16 [262144, 4096], P(('grp', 'mem')), may hold values from -0.09375 to 0.09375
- re_features: bfloat16 [262144, 256], P(('grp', 'mem')), may hold values from -6 to 6
- member_id: int32 [262144], P(('grp', 'mem')), may hold values from 0 to 2047, as said below
- slot: int32 [262144], P(('grp', 'mem')), may hold values from 0 to 2047, as said below
- labels: int32 [262144], P(('grp', 'mem')), may hold values 0 or 1
- offsets: float32 [262144], P(('grp', 'mem')), may hold values from -6 to 6
- feature_scale: float32 [4096], replicated, may hold values from 0.3 to 3
- w_start: float32 [4096], replicated, may hold values from -4 to 4
Outputs:
- fixed_weights: float32 [4096], replicated
- member_coef: float32 [2048, 256], P(('grp', 'mem'))
- row_offsets: float32 [262144], P(('grp', 'mem'))
The draws below stay inside these ranges and needn't reach their ends.
Inputs may be any that keep to these rules, and one draw needn't show every extreme that they name: A row of device k (devices counted along grp, then mem) belongs to group k // 32: member_id // 256 is that group, and (member_id mod 256) // 8 equals slot // 64. Rows per member are uneven. Within one device's rows the slots are distinct; slot // 64 is the mem index that owns the row's member, so at most 64 rows of one device go to one owner, and in every group one owner receives exactly 64 rows from every device of the group.
All inputs are finite; a program needn't handle non-finite values. No bound on the sum of `labels` on one device may be relied on, other than what follows from the above.
Results may differ from the reference program's by a relative error of at most 0.0003.
Values may be sent and summed in bfloat16 or wider, within the bound.
No kernel may reach another device: no remote copies, remote signals or barrier semaphores. Data moves between devices by JAX's collectives and lax.ppermute only.
A program may use at most 64 MiB of HBM per device.

```python
import math
import jax
import jax.numpy as jnp
from jax import lax

F = 4096
FR = 256
ROWS_DEV = 1024
MEM_DEV = 8
NEWTON = 2
CG_ITERS = 3
ROWS = 262144
CAP = 64
SLOTS = 2048
GROUP_MEMBERS = 256
MEMBERS = 2048
N_GRP = 8
N_MEM = 32


def layout_rows(key):
    base = jax.random.fold_in(key, 7001)

    def one_block(block_key, block):
        group = block // N_MEM
        group_key = jax.random.fold_in(base, 500000 + group)
        key_noise, key_rows, key_first, key_second = jax.random.split(block_key, 4)
        ranking = jax.random.permutation(group_key, N_MEM).astype(jnp.int32)
        owner_of = jnp.arange(SLOTS, dtype=jnp.int32) // CAP
        rank_of = ranking[owner_of]
        noise = jax.random.randint(key_noise, (SLOTS,), 0, 4096, dtype=jnp.int32)
        priority = jnp.where(rank_of == 0, noise - 4096, noise * (1 + rank_of))
        keyed = priority * SLOTS + jnp.arange(SLOTS, dtype=jnp.int32)
        picked = jnp.argsort(keyed)[:ROWS_DEV].astype(jnp.int32)
        shuffle = jax.random.permutation(key_rows, ROWS_DEV).astype(jnp.int32)
        slot_rows = picked[shuffle]
        local_id = jnp.minimum(jax.random.randint(key_first, (ROWS_DEV,), 0, MEM_DEV, dtype=jnp.int32), jax.random.randint(key_second, (ROWS_DEV,), 0, MEM_DEV, dtype=jnp.int32))
        member_rows = group * GROUP_MEMBERS + slot_rows // CAP * MEM_DEV + local_id
        return (member_rows.astype(jnp.int32), slot_rows)
    block_keys = jax.random.split(base, N_GRP * N_MEM)
    members, slots = jax.vmap(one_block)(block_keys, jnp.arange(N_GRP * N_MEM, dtype=jnp.int32))
    return (members.reshape(-1), slots.reshape(-1))


def draw_member_id(key, part):
    return layout_rows(key)[0]


def draw_slot(key, part):
    return layout_rows(key)[1]


def with_ends(values, rng, smallest, top_value):
    longest = values.shape.index(max(values.shape))
    spots = []
    for shift in (0, 1):
        where = [jax.random.randint(jax.random.fold_in(rng, axis), (), 0, length) for axis, length in enumerate(values.shape)]
        where[longest] = (where[longest] + shift) % values.shape[longest]
        spots.append(tuple(where))
    return values.at[spots[0]].set(smallest).at[spots[1]].set(top_value)


def levels(key, extent, pieces, low, top_value):
    level = 1.0
    for axis_at, shards_of in pieces:
        steps = jax.random.uniform(jax.random.fold_in(jax.random.fold_in(key, 6), axis_at), (shards_of,), jnp.float32, low / len(pieces), top_value / len(pieces))
        level = level * jnp.repeat(jnp.exp(steps), extent[axis_at] // shards_of).reshape((-1,) + (1,) * (len(extent) - 1 - axis_at))
    return level


def normal_values(rng, dims, scale, reach, cuts=(), held_as=jnp.bfloat16):
    gain = levels(rng, dims, cuts, -0.22, 0.18) if cuts else 1.0
    array = jax.random.normal(rng, dims, jnp.float32) * scale * gain
    return jnp.minimum(jnp.maximum(array, -reach), reach).astype(held_as)


def setup_inputs(seed: int = 0) -> dict:
    splits = jax.random.split(jax.random.key(seed), 9)
    return {
        "features": normal_values(splits[0], (ROWS, F), F ** -0.5, 0.09375, ((0, 256),)),
        "re_features": normal_values(splits[1], (ROWS, FR), 1.0, 6.0, ((0, 256),)),
        "member_id": draw_member_id(jax.random.fold_in(splits[8], 71), 0),
        "slot": draw_slot(jax.random.fold_in(splits[8], 71), 0),
        "labels": with_ends((jax.random.randint(splits[4], (ROWS,), 0, 2) < 1).astype(jnp.int32), jax.random.fold_in(splits[4], 1), 0, 1),
        "offsets": normal_values(splits[5], (ROWS,), 1.0, 6.0, ((0, 256),), jnp.float32),
        "feature_scale": jnp.clip(jnp.exp(jax.random.uniform(splits[6], (F,), jnp.float32, math.log(0.3), math.log(3.0))), 0.3, 3.0),
        "w_start": normal_values(splits[7], (F,), 0.5, 4.0, (), jnp.float32),
    }


ridge_fixed = 1.0
ridge_member = 1.0

def split_pair(values):
    upper_part = values.astype(jnp.bfloat16)
    held_part = lax.optimization_barrier(upper_part)
    lower_part = (values - held_part.astype(jnp.float32)).astype(jnp.bfloat16)
    return (upper_part, lower_part)

def split_two(vector):
    upper_part, lower_part = split_pair(vector)
    return jnp.stack([upper_part, lower_part], axis=1)

def apply_rows(features, vector):
    return jnp.sum(jnp.dot(features.astype(jnp.float32), split_two(vector).astype(jnp.float32), preferred_element_type=jnp.float32), axis=1)

def apply_columns(features, values):
    pair_cols = split_two(values)
    product = lax.dot_general(pair_cols.astype(jnp.float32), features.astype(jnp.float32), (((0,), (0,)), ((), ())), preferred_element_type=jnp.float32)
    return jnp.sum(product, axis=0)

def inner_rows(left, right):
    return lax.dot_general(left.astype(jnp.float32), right.astype(jnp.float32), (((0,), (0,)), ((), ())), preferred_element_type=jnp.float32)

def fit_members(received, arrived):
    curv_row = arrived[0]
    resid_row = arrived[1]
    local_row = arrived[2]
    onehot = (local_row[:, None] == jnp.arange(MEM_DEV).astype(arrived.dtype)[None, :]).astype(arrived.dtype)
    z_float = received.astype(jnp.float32)

    def gram_one(column):
        upper_part, lower_part = split_pair(z_float * (curv_row * column)[:, None])
        return inner_rows(received, upper_part) + inner_rows(received, lower_part)
    gram_all = lax.map(gram_one, onehot.T) + ridge_member * jnp.eye(received.shape[1], dtype=jnp.float32)
    grad_upper, grad_lower = split_pair(resid_row[:, None] * onehot)
    member_grad = inner_rows(grad_upper, received) + inner_rows(grad_lower, received)
    factor = jnp.linalg.cholesky(gram_all)
    member_coef = -jax.scipy.linalg.cho_solve((factor, True), member_grad[:, :, None])[:, :, 0]
    coef_upper, coef_lower = split_pair(member_coef)
    scores = jnp.dot(received.astype(jnp.float32), coef_upper.T.astype(jnp.float32), preferred_element_type=jnp.float32) + jnp.dot(received.astype(jnp.float32), coef_lower.T.astype(jnp.float32), preferred_element_type=jnp.float32)
    return (member_coef, jnp.sum(scores * onehot, axis=1))

def reference(features, re_features, member_id, slot, labels, offsets, feature_scale, w_start):
    target = labels.astype(jnp.float32)
    weights = w_start
    for newton_step in range(NEWTON):
        margin = apply_rows(features, feature_scale * weights) + offsets
        probability = jax.nn.sigmoid(margin)
        curvature = probability * (1.0 - probability)
        gradient = feature_scale * apply_columns(features, probability - target) + ridge_fixed * weights
        residual = -gradient
        direction = residual
        res_norm = jnp.sum(residual * residual)
        update = jnp.zeros_like(weights)
        for cg_step in range(CG_ITERS):
            inner = curvature * apply_rows(features, feature_scale * direction)
            hess_image = feature_scale * apply_columns(features, inner) + ridge_fixed * direction
            step_size = res_norm / jnp.sum(direction * hess_image)
            update = update + step_size * direction
            residual = residual - step_size * hess_image
            next_norm = jnp.sum(residual * residual)
            direction = residual + next_norm / res_norm * direction
            res_norm = next_norm
        weights = weights + update
    score = apply_rows(features, feature_scale * weights)
    probability = jax.nn.sigmoid(score)
    curvature = probability * (1.0 - probability)
    resid_row = probability - target
    local_id = (member_id % MEM_DEV).astype(jnp.float32)
    row_weights = jnp.stack([curvature, resid_row, local_id], axis=1)
    device_of = (jnp.arange(ROWS, dtype=jnp.int32) // ROWS_DEV).astype(jnp.int32)
    flat_slot = (device_of * SLOTS + slot).astype(jnp.int32)
    owners_all = N_GRP * N_MEM
    z_buffer = jnp.zeros((owners_all * SLOTS, FR), re_features.dtype).at[flat_slot].set(re_features)
    w_buffer = jnp.zeros((owners_all * SLOTS, 3), jnp.float32).at[flat_slot].set(row_weights)
    z_owner = z_buffer.reshape(N_GRP, N_MEM, N_MEM, CAP, FR).transpose(0, 2, 1, 3, 4).reshape(owners_all, SLOTS, FR)
    w_owner = w_buffer.reshape(N_GRP, N_MEM, N_MEM, CAP, 3).transpose(0, 2, 1, 3, 4).reshape(owners_all, SLOTS, 3)
    all_coef, slot_scores = lax.map(lambda pair_in: fit_members(pair_in[0], pair_in[1].T), (z_owner, w_owner))
    back_flat = slot_scores.reshape(N_GRP, N_MEM, N_MEM, CAP).transpose(0, 2, 1, 3).reshape(-1)
    row_offsets = back_flat[flat_slot]
    return (weights, all_coef.reshape(MEMBERS, FR), row_offsets)
```

```python
import functools
import jax
import jax.numpy as jnp
from jax import lax
from jax.experimental import pallas as pl
from jax.experimental.pallas import tpu as pltpu
from jax.sharding import Mesh, PartitionSpec as P

MEM_DEV = 8
NEWTON = 2
RIDGE = 1.0
TILE = 256
PANEL = 16
F32 = jnp.float32
BF16 = jnp.bfloat16
HIGH = lax.Precision.HIGHEST


def dot_nn(a, b, precision=None):
    return lax.dot_general(a, b, (((1,), (0,)), ((), ())), precision=precision,
                           preferred_element_type=F32)


def dot_nt(a, b, precision=None):
    return lax.dot_general(a, b, (((1,), (1,)), ((), ())), precision=precision,
                           preferred_element_type=F32)


def dot_tn(a, b, precision=None):
    return lax.dot_general(a, b, (((0,), (0,)), ((), ())), precision=precision,
                           preferred_element_type=F32)


def split_rows(row):
    high = row.astype(BF16).astype(F32)
    low = row - high
    at = lax.broadcasted_iota(jnp.int32, (8, row.shape[1]), 0)
    return jnp.where(at == 0, high, jnp.where(at == 1, low, 0.0)).astype(BF16)


def sigmoid(x):
    return 1.0 / (1.0 + jnp.exp(-x))


def total(row):
    return jnp.sum(row, axis=1, keepdims=True)


def sum_parts(ref):
    acc = ref[0]
    for i in range(1, ref.shape[0]):
        acc = acc + ref[i]
    return acc


def forward(xs, x_ref):
    both = dot_nt(xs, x_ref[...])
    return both[0:1] + both[1:2]


def backward(row, x_ref, acc):
    acc[...] += dot_nn(split_rows(row), x_ref[...])


def finish(acc, out_ref):
    val = acc[0:1] + acc[1:2]
    for i in range(out_ref.shape[0]):
        out_ref[i] = val


def grad_first_kernel(x_ref, scale_ref, w_ref, off_ref, lab_ref,
                      out_ref, score_ref, curv_ref, xs, acc):
    step = pl.program_id(0)

    @pl.when(step == 0)
    def _():
        xs[...] = split_rows(scale_ref[...] * w_ref[...])
        acc[...] = jnp.zeros_like(acc)

    score = forward(xs[...], x_ref)
    prob = sigmoid(score + off_ref[...])
    score_ref[...] = score
    curv_ref[...] = prob * (1.0 - prob)
    backward(prob - lab_ref[...], x_ref, acc)

    @pl.when(step == pl.num_programs(0) - 1)
    def _():
        finish(acc, out_ref)


def grad_next_kernel(x_ref, part_ref, rr_ref, w_ref, u_ref, p_ref, score_ref, t_ref, m_ref,
                     off_ref, lab_ref,
                     out_ref, w_out, score_out, curv_ref, coef, acc):
    step = pl.program_id(0)

    @pl.when(step == 0)
    def _():
        p = p_ref[...]
        php = jnp.sum(part_ref[:, 0, :], axis=0, keepdims=True)[:, 0:1] + RIDGE * total(p * p)
        a = rr_ref[:, 0:1] / php
        coef[...] = jnp.broadcast_to(a, coef.shape)
        w_out[...] = w_ref[...] + (u_ref[...] + a * p)
        acc[...] = jnp.zeros_like(acc)

    score = score_ref[...] + (m_ref[...] + coef[:, 0:1] * t_ref[...])
    prob = sigmoid(score + off_ref[...])
    score_out[...] = score
    curv_ref[...] = prob * (1.0 - prob)
    backward(prob - lab_ref[...], x_ref, acc)

    @pl.when(step == pl.num_programs(0) - 1)
    def _():
        finish(acc, out_ref)


def cg_first_kernel(x_ref, sum_ref, scale_ref, w_ref, curv_ref,
                    out_ref, p_out, rr_out, t_ref, xs, acc):
    step = pl.program_id(0)

    @pl.when(step == 0)
    def _():
        r = -(scale_ref[...] * sum_parts(sum_ref) + RIDGE * w_ref[...])
        p_out[...] = r
        rr_out[...] = jnp.broadcast_to(total(r * r), rr_out.shape)
        xs[...] = split_rows(scale_ref[...] * r)
        acc[...] = jnp.zeros_like(acc)

    t = forward(xs[...], x_ref)
    t_ref[...] = t
    backward(curv_ref[...] * t, x_ref, acc)

    @pl.when(step == pl.num_programs(0) - 1)
    def _():
        finish(acc, out_ref)


def cg_update(sum_ref, scale_ref, p_ref, r_ref, u_ref, rr_ref, p_out, r_out, u_out, rr_out,
              coef, xs):
    p = p_ref[...]
    q = scale_ref[...] * sum_parts(sum_ref) + RIDGE * p
    rr = rr_ref[:, 0:1]
    a = rr / total(p * q)
    u = a * p if u_ref is None else u_ref[...] + a * p
    r = r_ref[...] - a * q
    nn = total(r * r)
    p = r + (nn / rr) * p
    u_out[...] = u
    if r_out is not None:
        r_out[...] = r
    p_out[...] = p
    rr_out[...] = jnp.broadcast_to(nn, rr_out.shape)
    coef[...] = jnp.broadcast_to(a, coef.shape)
    xs[...] = split_rows(scale_ref[...] * p)


def cg_next_kernel(x_ref, sum_ref, scale_ref, curv_ref, p_ref, rr_ref, t_in,
                   out_ref, p_out, r_out, u_out, rr_out, t_ref, m_ref, coef, xs, acc):
    step = pl.program_id(0)

    @pl.when(step == 0)
    def _():
        cg_update(sum_ref, scale_ref, p_ref, p_ref, None, rr_ref, p_out, r_out, u_out, rr_out,
                  coef, xs)
        acc[...] = jnp.zeros_like(acc)

    m_ref[...] = coef[:, 0:1] * t_in[...]
    t = forward(xs[...], x_ref)
    t_ref[...] = t
    backward(curv_ref[...] * t, x_ref, acc)

    @pl.when(step == pl.num_programs(0) - 1)
    def _():
        finish(acc, out_ref)


def cg_last_step(x_ref, sum_ref, scale_ref, curv_ref, p_ref, r_ref, u_ref, rr_ref, t_in, m_in,
                 p_out, u_out, rr_out, t_ref, m_ref, coef, xs, acc):
    step = pl.program_id(0)

    @pl.when(step == 0)
    def _():
        cg_update(sum_ref, scale_ref, p_ref, r_ref, u_ref, rr_ref, p_out, None, u_out, rr_out,
                  coef, xs)
        acc[...] = jnp.zeros_like(acc)

    m_ref[...] = m_in[...] + coef[:, 0:1] * t_in[...]
    t = forward(xs[...], x_ref)
    t_ref[...] = t
    acc[...] += jnp.broadcast_to(total(curv_ref[...] * t * t), acc.shape)


def cg_last_kernel(x_ref, sum_ref, scale_ref, curv_ref, p_ref, r_ref, u_ref, rr_ref, t_in, m_in,
                   out_ref, p_out, u_out, rr_out, t_ref, m_ref, coef, xs, acc):
    cg_last_step(x_ref, sum_ref, scale_ref, curv_ref, p_ref, r_ref, u_ref, rr_ref, t_in, m_in,
                 p_out, u_out, rr_out, t_ref, m_ref, coef, xs, acc)

    @pl.when(pl.program_id(0) == pl.num_programs(0) - 1)
    def _():
        out_ref[...] = jnp.broadcast_to(acc[0:1, :].reshape(1, 1, 128), out_ref.shape)


def owner_hot(slot, owners, cap):
    rows = lax.broadcasted_iota(jnp.int32, (owners, slot.shape[1]), 0)
    hot_owner = jnp.where(rows == slot // cap, 1.0, 0.0)
    lanes = lax.broadcasted_iota(jnp.int32, (cap, slot.shape[1]), 0)
    hot_cap = jnp.where(lanes == slot % cap, 1.0, 0.0)
    return hot_owner, hot_cap


def pack_rows(row, hot_owner, hot_cap):
    return dot_nt(hot_owner * row, hot_cap, HIGH)


def cg_last_pack_kernel(x_ref, sum_ref, scale_ref, curv_ref, p_ref, r_ref, u_ref, rr_ref, t_in,
                        m_in, score_ref, slot_ref, code_ref,
                        out_ref, p_out, u_out, rr_out, t_ref, m_ref, coef, xs, acc, send):
    cg_last_step(x_ref, sum_ref, scale_ref, curv_ref, p_ref, r_ref, u_ref, rr_ref, t_in, m_in,
                 p_out, u_out, rr_out, t_ref, m_ref, coef, xs, acc)
    step = pl.program_id(0)
    owners, cap = out_ref.shape[0], send.shape[1] // 4

    @pl.when(step == 0)
    def _():
        send[...] = jnp.zeros_like(send)

    hot_owner, hot_cap = owner_hot(slot_ref[...], owners, cap)
    send[:, 0:cap] += pack_rows(score_ref[...] + m_ref[...], hot_owner, hot_cap)
    send[:, cap:2 * cap] += pack_rows(t_ref[...], hot_owner, hot_cap)
    send[:, 2 * cap:3 * cap] += pack_rows(code_ref[...], hot_owner, hot_cap)

    @pl.when(step == pl.num_programs(0) - 1)
    def _():
        send[:, 3 * cap:] = jnp.broadcast_to(acc[0:1, 0:cap], (owners, cap))
        for i in range(owners):
            out_ref[i] = send[i:i + 1, :]


def z_pack_kernel(slot_ref, z_ref, out_ref):
    block = out_ref.shape[0]
    first = pl.program_id(0) * block
    rows = lax.broadcasted_iota(jnp.int32, (block, slot_ref.shape[1]), 0) + first
    hot = jnp.where(rows == slot_ref[...], 1.0, 0.0).astype(BF16)
    out_ref[...] = dot_nn(hot, z_ref[...]).astype(BF16)


def three_parts(v):
    a = v.astype(BF16)
    rest = v - a.astype(F32)
    b = rest.astype(BF16)
    c = (rest - b.astype(F32)).astype(BF16)
    return a, b, c


def get_lanes(halves, rows, lane):
    if lane:
        return halves[1][rows, :]
    return jnp.concatenate([halves[0][rows, :], halves[1][rows, :]], axis=1)


def put_lanes(halves, rows, lane, value):
    if lane:
        halves[1][rows, :] = value
    else:
        halves[0][rows, :] = value[:, :128]
        halves[1][rows, :] = value[:, 128:]


def member_kernel(z_ref, arr_ref, part_ref, rr_ref, w_ref, u_ref, p_ref,
                  w_out, coef_ref, back_ref,
                  base, tvec, code, zt, hi, lo, mat0, mat1, red0, red1):
    owners = arr_ref.shape[0]
    cap = arr_ref.shape[2] // 4
    fr = z_ref.shape[1]
    slots = z_ref.shape[0]
    p = p_ref[...]
    php = jnp.sum(part_ref[:, 0, :], axis=0, keepdims=True)[:, 0:1] + RIDGE * total(p * p)
    a = rr_ref[:, 0:1] / php
    w_out[...] = w_ref[...] + (u_ref[...] + a * p)
    for o in range(owners):
        got = arr_ref[o]
        base[:, o * cap:(o + 1) * cap] = got[:, 0:cap]
        tvec[:, o * cap:(o + 1) * cap] = got[:, cap:2 * cap]
        code[:, o * cap:(o + 1) * cap] = got[:, 2 * cap:3 * cap]
    prob = sigmoid(base[...] + a * tvec[...])
    curv = prob * (1.0 - prob)
    codes = code[...]
    label = jnp.where(codes >= 24.0, 1.0, 0.0)
    resid = prob - label
    local = codes - 16.0 - 8.0 * label
    at = lax.broadcasted_iota(jnp.int32, (MEM_DEV, slots), 0).astype(F32)
    onehot = jnp.where(local == at, 1.0, 0.0)

    z_t = z_ref[...].T
    zt[...] = z_t
    chunk = 512
    for c in range(0, slots, chunk):
        cz = zt[:, c:c + chunk].astype(F32) * curv[:, c:c + chunk]
        high = cz.astype(BF16)
        hi[:, c:c + chunk] = high
        lo[:, c:c + chunk] = (cz - high.astype(F32)).astype(BF16)
    mat, red = (mat0, mat1), (red0, red1)
    eye = jnp.where(lax.broadcasted_iota(jnp.int32, (fr, fr), 0)
                    == lax.broadcasted_iota(jnp.int32, (fr, fr), 1), RIDGE, 0.0)
    for m in range(MEM_DEV):
        mask = onehot[m:m + 1].astype(BF16)
        gram = dot_nn(hi[...] * mask, z_ref[...]) + dot_nn(lo[...] * mask, z_ref[...])
        put_lanes(mat, slice(m * fr, (m + 1) * fr), 0, gram + eye)
    rm = resid * onehot
    rm_high = rm.astype(BF16)
    rm_low = (rm - rm_high.astype(F32)).astype(BF16)
    rhs = dot_nn(rm_high, z_ref[...]) + dot_nn(rm_low, z_ref[...])

    for k0 in range(0, fr, PANEL):
        lane0 = (k0 // 128) * 128
        orig = [get_lanes(mat, pl.ds(k0 + i, MEM_DEV, stride=fr), lane0) for i in range(PANEL)]
        rows = list(orig)
        ys = [rhs[:, k0 + i:k0 + i + 1] for i in range(PANEL)]
        for kk in range(PANEL):
            k = k0 + kk - lane0
            inv = 1.0 / rows[kk][:, k:k + 1]
            rows[kk] = rows[kk] * inv
            ys[kk] = ys[kk] * inv
            for i in range(PANEL):
                if i != kk:
                    f = rows[i][:, k:k + 1]
                    rows[i] = rows[i] - f * rows[kk]
                    ys[i] = ys[i] - f * ys[kk]
        tail = rhs[:, lane0:]
        lanes = lax.broadcasted_iota(jnp.int32, tail.shape, 1) + lane0
        drop = jnp.zeros_like(tail)
        place = tail
        for i in range(PANEL):
            drop = drop + orig[i] * ys[i]
            place = jnp.where(lanes == k0 + i, ys[i], place)
        tail = jnp.where(lanes >= k0 + PANEL, tail - drop, place)
        rhs = tail if lane0 == 0 else jnp.concatenate([rhs[:, :lane0], tail], axis=1)
        for i in range(PANEL):
            put_lanes(red, slice((k0 + i) * MEM_DEV, (k0 + i + 1) * MEM_DEV), lane0, rows[i])
        top = k0 + PANEL
        if top < fr:
            lane1 = (top // 128) * 128
            row1 = lane1
            for m in range(MEM_DEV):
                o = get_lanes(mat, slice(m * fr + k0, m * fr + k0 + PANEL), row1)
                w = get_lanes(red, pl.ds(k0 * MEM_DEV + m, PANEL, stride=MEM_DEV), lane1)
                o1, o2, o3 = three_parts(o)
                w1, w2, w3 = three_parts(w)
                left = jnp.concatenate([o1, o1, o2, o2, o1, o3], axis=0)
                right = jnp.concatenate([w1, w2, w1, w2, w3, w1], axis=0)
                rest = slice(m * fr + row1, (m + 1) * fr)
                put_lanes(mat, rest, lane1, get_lanes(mat, rest, lane1) - dot_tn(left, right))

    lanes = lax.broadcasted_iota(jnp.int32, rhs.shape, 1)
    sol = jnp.where(lanes >= fr - PANEL, rhs, 0.0)
    for k0 in range(fr - 2 * PANEL, -1, -PANEL):
        new = sol
        lane0 = (k0 // 128) * 128
        for i in range(PANEL):
            w = get_lanes(red, slice((k0 + i) * MEM_DEV, (k0 + i + 1) * MEM_DEV), lane0)
            d = jnp.sum(w * sol[:, lane0:], axis=1, keepdims=True)
            new = jnp.where(lanes == k0 + i, rhs - d, new)
        sol = new
    coef = -sol
    coef_ref[...] = coef
    chigh = coef.astype(BF16)
    clow = (coef - chigh.astype(F32)).astype(BF16)
    scores = dot_nn(chigh, zt[...]) + dot_nn(clow, zt[...])
    back = jnp.sum(scores * onehot, axis=0, keepdims=True)
    for o in range(owners):
        back_ref[o] = back[:, o * cap:(o + 1) * cap]


def unpack_kernel(back_ref, slot_ref, out_ref):
    owners, _, cap = back_ref.shape
    back = back_ref[:, 0, :]
    hot_owner, hot_cap = owner_hot(slot_ref[...], owners, cap)
    rows = dot_tn(back, hot_owner, HIGH)
    out_ref[...] = jnp.sum(rows * hot_cap, axis=0, keepdims=True)


VMEM_LIMIT = 48 * 1024 * 1024


def whole(shape):
    return pl.BlockSpec(shape, lambda i: (0,) * len(shape))


def rows_spec():
    return pl.BlockSpec((1, TILE), lambda i: (0, i))


def streamed(kernel, features, ins, outs, scratch, name):
    rows, f = features.shape
    in_specs = [pl.BlockSpec((TILE, f), lambda i: (i, 0))]
    for v, cut in ins:
        in_specs.append(rows_spec() if cut else whole(v.shape))
    out_specs = [rows_spec() if cut else whole(s) for s, cut in outs]
    return pl.pallas_call(
        kernel,
        grid=(rows // TILE,),
        in_specs=in_specs,
        out_specs=out_specs,
        out_shape=[jax.ShapeDtypeStruct(s, F32) for s, _ in outs],
        scratch_shapes=scratch,
        compiler_params=pltpu.CompilerParams(vmem_limit_bytes=VMEM_LIMIT),
        name=name,
    )(features, *[v for v, _ in ins])


PH1 = ("core", "z")
PH2 = ("x", "y")


def on_device(features, re_features, member_id, slot, labels, offsets, feature_scale, w_start,
              *, sizes):
    n1 = sizes["core"] * sizes["z"]
    n2 = sizes["x"] * sizes["y"]
    n_mem = sizes["y"] * sizes["z"]
    n_grp = sizes["x"] * sizes["core"]
    rows, f = features.shape
    fr = re_features.shape[1]
    slots = 2 * rows
    cap = slots // n_mem
    slot_row = slot.reshape(1, rows)
    lab = labels.astype(F32).reshape(1, rows)
    off = offsets.reshape(1, rows)
    scale = feature_scale.reshape(1, f)
    w = w_start.reshape(1, f)
    code = (member_id % MEM_DEV + 8 * labels + 16).astype(F32).reshape(1, rows)

    def exchange(v, axes):
        return lax.all_to_all(v, axes, 0, 0, tiled=True)

    def reduce_rest(parts):
        got = exchange(parts, PH1)
        mid = jnp.sum(got, axis=0)
        return exchange(jnp.broadcast_to(mid[None], (n2, 1, f)), PH2)

    zblk = 256
    packed = pl.pallas_call(
        z_pack_kernel,
        grid=(slots // zblk,),
        in_specs=[whole((1, rows)), whole((rows, fr))],
        out_specs=pl.BlockSpec((zblk, fr), lambda i: (i, 0)),
        out_shape=jax.ShapeDtypeStruct((slots, fr), BF16),
        name="z_pack",
    )(slot_row, re_features)
    z_got = lax.all_to_all(packed.reshape(n_mem, cap, fr), ("y", "z"), 0, 0, tiled=True)
    z_got = z_got.reshape(slots, fr)

    vec = ((1, f), False)
    small = ((1, 128), False)
    row = ((1, rows), True)
    parts = ((n1, 1, f), False)
    xs = pltpu.VMEM((8, f), BF16)
    acc = pltpu.VMEM((8, f), F32)
    coef = pltpu.VMEM((1, 128), F32)
    one = pltpu.VMEM((8, 128), F32)

    gpart, score, curv = streamed(
        grad_first_kernel, features,
        [(scale, False), (w, False), (off, True), (lab, True)],
        [parts, row, row], [xs, acc], "grad_first")
    for it in range(NEWTON):
        g2 = reduce_rest(gpart)
        hpart, p, rr, t = streamed(
            cg_first_kernel, features,
            [(g2, False), (scale, False), (w, False), (curv, True)],
            [parts, vec, small, row], [xs, acc], "cg_first")
        h2 = reduce_rest(hpart)
        hpart, p, r, u, rr, t, m = streamed(
            cg_next_kernel, features,
            [(h2, False), (scale, False), (curv, True), (p, False), (rr, False), (t, True)],
            [parts, vec, vec, vec, small, row, row], [coef, xs, acc], "cg_next")
        h2 = reduce_rest(hpart)
        ins = [(h2, False), (scale, False), (curv, True), (p, False), (r, False), (u, False),
               (rr, False), (t, True), (m, True)]
        outs = [vec, vec, small, row, row]
        if it + 1 < NEWTON:
            n_all = n1 * n2
            spart, p, u, rr, t, m = streamed(
                cg_last_kernel, features, ins, [((n_all, 1, 128), False)] + outs,
                [coef, xs, one], "cg_last")
            sgot = exchange(spart, ("x", "core", "y", "z"))
            gpart, w, score, curv = streamed(
                grad_next_kernel, features,
                [(sgot, False), (rr, False), (w, False), (u, False), (p, False), (score, True),
                 (t, True), (m, True), (off, True), (lab, True)],
                [parts, vec, row, row], [coef, acc], "grad_next")
        else:
            send, p, u, rr, t, m = streamed(
                cg_last_pack_kernel, features,
                ins + [(score, True), (slot_row, True), (code, True)],
                [((n_mem, 1, 4 * cap), False)] + outs,
                [coef, xs, one, pltpu.VMEM((n_mem, 4 * cap), F32)], "cg_last_pack")
    got = exchange(send, ("y", "z"))
    part = jnp.sum(got[:, 0, 3 * cap])
    part = exchange(jnp.broadcast_to(part, (n_grp, 1, 128)), ("x", "core"))
    w, member_coef, back = pl.pallas_call(
        member_kernel,
        out_shape=[jax.ShapeDtypeStruct((1, f), F32),
                   jax.ShapeDtypeStruct((MEM_DEV, fr), F32),
                   jax.ShapeDtypeStruct((n_mem, 1, cap), F32)],
        scratch_shapes=[pltpu.VMEM((1, slots), F32)] * 3
        + [pltpu.VMEM((fr, slots), BF16)] * 3
        + [pltpu.VMEM((MEM_DEV * fr, 128), F32)] * 4,
        compiler_params=pltpu.CompilerParams(vmem_limit_bytes=VMEM_LIMIT),
        name="members",
    )(z_got, got, part, rr, w, u, p)
    returned = exchange(back, ("y", "z"))
    row_offsets = pl.pallas_call(
        unpack_kernel,
        out_shape=jax.ShapeDtypeStruct((1, rows), F32),
        compiler_params=pltpu.CompilerParams(vmem_limit_bytes=VMEM_LIMIT),
        name="unpack",
    )(returned, slot_row)
    return (w.reshape(f), member_coef, row_offsets.reshape(rows))


def solution(mesh):
    n_grp, n_mem = mesh.shape["grp"], mesh.shape["mem"]
    shape = {"x": n_grp // 2, "core": 2, "y": 4, "z": n_mem // 4}
    fine = Mesh(mesh.devices.reshape(tuple(shape.values())), tuple(shape))
    cut = P(("x", "core", "y", "z"))
    cut2 = P(("x", "core", "y", "z"), None)
    return jax.shard_map(
        functools.partial(on_device, sizes=shape),
        mesh=fine,
        in_specs=(cut2, cut2, cut, cut, cut, cut, P(), P()),
        out_specs=(P(), cut2, cut),
        check_vma=False,
    )
```

```python
import functools
import jax
import jax.numpy as jnp
from jax import lax
from jax.experimental import pallas as pl
from jax.experimental.pallas import tpu as pltpu
from jax.sharding import Mesh, PartitionSpec as P

MEM_DEV = 8
NEWTON = 2
RIDGE = 1.0
PANEL = 16
BLOCK = 8
F32 = jnp.float32
BF16 = jnp.bfloat16
HIGH = lax.Precision.HIGHEST


def dot_nn(a, b, precision=None):
    return lax.dot_general(a, b, (((1,), (0,)), ((), ())), precision=precision,
                           preferred_element_type=F32)


def dot_nt(a, b, precision=None):
    return lax.dot_general(a, b, (((1,), (1,)), ((), ())), precision=precision,
                           preferred_element_type=F32)


def dot_tn(a, b, precision=None):
    return lax.dot_general(a, b, (((0,), (0,)), ((), ())), precision=precision,
                           preferred_element_type=F32)


def split_rows(row):
    high = row.astype(BF16).astype(F32)
    low = row - high
    at = lax.broadcasted_iota(jnp.int32, (8, row.shape[1]), 0)
    return jnp.where(at == 0, high, jnp.where(at == 1, low, 0.0)).astype(BF16)


def sigmoid(x):
    return 1.0 / (1.0 + jnp.exp(-x))


def total(row):
    return jnp.sum(row, axis=1, keepdims=True)


def sum_parts(ref):
    acc = ref[0]
    for i in range(1, ref.shape[0]):
        acc = acc + ref[i]
    return acc


def forward(xs, x_ref):
    both = dot_nt(xs, x_ref[...])
    return both[0:1] + both[1:2]


def backward(row, x_ref, out_ref):
    both = dot_nn(split_rows(row), x_ref[...])
    val = both[0:1] + both[1:2]
    for i in range(out_ref.shape[0]):
        out_ref[i] = val


def grad_first_kernel(x_ref, scale_ref, w_ref, off_ref, lab_ref, out_ref, score_ref, curv_ref):
    score = forward(split_rows(scale_ref[...] * w_ref[...]), x_ref)
    prob = sigmoid(score + off_ref[...])
    score_ref[...] = score
    curv_ref[...] = prob * (1.0 - prob)
    backward(prob - lab_ref[...], x_ref, out_ref)


def grad_next_kernel(x_ref, part_ref, rr_ref, w_ref, u_ref, p_ref, score_ref, t_ref, m_ref,
                     off_ref, lab_ref, out_ref, w_out, score_out, curv_ref):
    a = last_coef(part_ref, rr_ref, p_ref)
    w_out[...] = w_ref[...] + (u_ref[...] + a * p_ref[...])
    score = score_ref[...] + (m_ref[...] + a * t_ref[...])
    prob = sigmoid(score + off_ref[...])
    score_out[...] = score
    curv_ref[...] = prob * (1.0 - prob)
    backward(prob - lab_ref[...], x_ref, out_ref)


def last_coef(part_ref, rr_ref, p_ref):
    p = p_ref[...]
    php = jnp.sum(part_ref[:, 0, :], axis=0, keepdims=True)[:, 0:1] + RIDGE * total(p * p)
    return rr_ref[:, 0:1] / php


def cg_first_kernel(x_ref, sum_ref, scale_ref, w_ref, curv_ref, out_ref, p_out, rr_out, t_ref):
    r = -(scale_ref[...] * sum_parts(sum_ref) + RIDGE * w_ref[...])
    p_out[...] = r
    rr_out[...] = jnp.broadcast_to(total(r * r), rr_out.shape)
    t = forward(split_rows(scale_ref[...] * r), x_ref)
    t_ref[...] = t
    backward(curv_ref[...] * t, x_ref, out_ref)


def cg_update(sum_ref, scale_ref, p_ref, r_ref, u_ref, rr_ref, p_out, r_out, u_out, rr_out):
    p = p_ref[...]
    q = scale_ref[...] * sum_parts(sum_ref) + RIDGE * p
    rr = rr_ref[:, 0:1]
    a = rr / total(p * q)
    u = a * p if u_ref is None else u_ref[...] + a * p
    r = r_ref[...] - a * q
    nn = total(r * r)
    p = r + (nn / rr) * p
    u_out[...] = u
    if r_out is not None:
        r_out[...] = r
    p_out[...] = p
    rr_out[...] = jnp.broadcast_to(nn, rr_out.shape)
    return a, split_rows(scale_ref[...] * p)


def cg_next_kernel(x_ref, sum_ref, scale_ref, curv_ref, p_ref, rr_ref, t_in,
                   out_ref, p_out, r_out, u_out, rr_out, t_ref, m_ref):
    a, xs = cg_update(sum_ref, scale_ref, p_ref, p_ref, None, rr_ref, p_out, r_out, u_out, rr_out)
    m_ref[...] = a * t_in[...]
    t = forward(xs, x_ref)
    t_ref[...] = t
    backward(curv_ref[...] * t, x_ref, out_ref)


def cg_last_kernel(x_ref, sum_ref, scale_ref, curv_ref, p_ref, r_ref, u_ref, rr_ref, t_in, m_in,
                   out_ref, p_out, u_out, rr_out, t_ref, m_ref):
    a, xs = cg_update(sum_ref, scale_ref, p_ref, r_ref, u_ref, rr_ref, p_out, None, u_out, rr_out)
    m_ref[...] = m_in[...] + a * t_in[...]
    t = forward(xs, x_ref)
    t_ref[...] = t
    out_ref[...] = jnp.broadcast_to(total(curv_ref[...] * t * t).reshape(1, 1, 1), out_ref.shape)


def owner_hot(slot, owners, cap):
    rows = lax.broadcasted_iota(jnp.int32, (owners, slot.shape[1]), 0)
    hot_owner = jnp.where(rows == slot // cap, 1.0, 0.0)
    lanes = lax.broadcasted_iota(jnp.int32, (cap, slot.shape[1]), 0)
    hot_cap = jnp.where(lanes == slot % cap, 1.0, 0.0)
    return hot_owner, hot_cap


def cg_last_pack_kernel(x_ref, sum_ref, scale_ref, curv_ref, p_ref, r_ref, u_ref, rr_ref, t_in,
                        m_in, score_ref, slot_ref, code_ref, out_ref, p_out, u_out, rr_out):
    a, xs = cg_update(sum_ref, scale_ref, p_ref, r_ref, u_ref, rr_ref, p_out, None, u_out, rr_out)
    owners, cap = out_ref.shape[0], out_ref.shape[2] // 4
    hot_owner, hot_cap = owner_hot(slot_ref[...], owners, cap)
    t = forward(xs, x_ref)
    done = score_ref[...] + (m_in[...] + a * t_in[...])
    php = total(curv_ref[...] * t * t)
    left = jnp.concatenate([hot_owner * done, hot_owner * t, hot_owner * code_ref[...]], axis=0)
    send = dot_nt(left, hot_cap, HIGH)
    part = jnp.broadcast_to(php, (1, cap))
    for i in range(owners):
        out_ref[i] = jnp.concatenate(
            [send[j * owners + i:j * owners + i + 1] for j in range(3)] + [part], axis=1)


def z_pack_kernel(slot_ref, z_ref, out_ref, buf, sems):
    block = buf.shape[1]
    copies = []
    for b in range(buf.shape[0]):
        rows = lax.broadcasted_iota(jnp.int32, (block, slot_ref.shape[1]), 0) + b * block
        hot = jnp.where(rows == slot_ref[...], 1.0, 0.0).astype(BF16)
        buf[b] = dot_nn(hot, z_ref[...]).astype(BF16)
        copies.append(pltpu.make_async_copy(
            buf.at[b], out_ref.at[pl.ds(b * block, block)], sems.at[b]))
        copies[-1].start()
    for copy in copies:
        copy.wait()


def again_kernel(sum_ref, out_ref):
    val = sum_parts(sum_ref)
    for i in range(out_ref.shape[0]):
        out_ref[i] = val


def part_kernel(arr_ref, out_ref):
    last = arr_ref.shape[2] - 1
    got = arr_ref[:, 0, :]
    val = jnp.sum(got, axis=0, keepdims=True)[:, last:]
    out_ref[...] = jnp.broadcast_to(val.reshape(1, 1, 1), out_ref.shape)


def three_parts(v):
    a = v.astype(BF16)
    rest = v - a.astype(F32)
    b = rest.astype(BF16)
    c = (rest - b.astype(F32)).astype(BF16)
    return a, b, c


def get_lanes(halves, rows, lane):
    if lane:
        return halves[1][rows, :]
    return jnp.concatenate([halves[0][rows, :], halves[1][rows, :]], axis=1)


def put_lanes(halves, rows, lane, value):
    if lane:
        halves[1][rows, :] = value
    else:
        halves[0][rows, :] = value[:, :128]
        halves[1][rows, :] = value[:, 128:]


def reduce_block(rows, lane, block, others):
    def at(i, j):
        return jnp.broadcast_to(rows[i][0][:, lane + j:lane + j + 1], rows[i][0].shape)

    block, others = list(block), list(others)
    c = {(i, j): at(i, j) for i in block for j in block if j <= i}
    far = {(i, j): at(i, j) for i in others for j in block}
    lower, inv = {}, {}
    for j in block:
        inv[j] = 1.0 / c[j, j]
        for i in block:
            if i > j:
                lower[i, j] = c[i, j] * inv[j]
        for i in block:
            for k in block:
                if j < k <= i:
                    c[i, k] = c[i, k] - lower[i, j] * c[k, j]
    for j in block:
        for i in block:
            if i > j:
                rows[i] = [v - lower[i, j] * w for v, w in zip(rows[i], rows[j])]
    for j in block:
        rows[j] = [w * inv[j] for w in rows[j]]
    for j in reversed(block):
        for i in block:
            if i < j:
                rows[i] = [v - lower[j, i] * w for v, w in zip(rows[i], rows[j])]
    for j in block:
        for i in others:
            rows[i] = [v - far[i, j] * w for v, w in zip(rows[i], rows[j])]


def member_kernel(z_hbm, arr_ref, part_ref, rr_ref, w_ref, u_ref, p_ref,
                  w_out, coef_ref, back_ref,
                  base, tvec, code, zt, hi, lo, mat0, mat1, red0, red1, z_ref, sem):
    copy = pltpu.make_async_copy(z_hbm, z_ref, sem)
    copy.start()
    owners = arr_ref.shape[0]
    cap = arr_ref.shape[2] // 4
    fr = z_ref.shape[1]
    slots = z_ref.shape[0]
    p = p_ref[...]
    php = jnp.sum(part_ref[:, 0, :], axis=0, keepdims=True)[:, 0:1] + RIDGE * total(p * p)
    a = rr_ref[:, 0:1] / php
    w_out[...] = w_ref[...] + (u_ref[...] + a * p)
    for o in range(owners):
        got = arr_ref[o]
        base[:, o * cap:(o + 1) * cap] = got[:, 0:cap]
        tvec[:, o * cap:(o + 1) * cap] = got[:, cap:2 * cap]
        code[:, o * cap:(o + 1) * cap] = got[:, 2 * cap:3 * cap]
    prob = sigmoid(base[...] + a * tvec[...])
    curv = prob * (1.0 - prob)
    codes = code[...]
    label = jnp.where(codes >= 24.0, 1.0, 0.0)
    resid = prob - label
    local = codes - 16.0 - 8.0 * label
    at = lax.broadcasted_iota(jnp.int32, (MEM_DEV, slots), 0).astype(F32)
    onehot = jnp.where(local == at, 1.0, 0.0)

    copy.wait()
    z_t = z_ref[...].T
    zt[...] = z_t
    chunk = 512
    for c in range(0, slots, chunk):
        cz = zt[:, c:c + chunk].astype(F32) * curv[:, c:c + chunk]
        high = cz.astype(BF16)
        hi[:, c:c + chunk] = high
        lo[:, c:c + chunk] = (cz - high.astype(F32)).astype(BF16)
    mat, red = (mat0, mat1), (red0, red1)
    eye = jnp.where(lax.broadcasted_iota(jnp.int32, (fr, fr), 0)
                    == lax.broadcasted_iota(jnp.int32, (fr, fr), 1), RIDGE, 0.0)
    for m in range(MEM_DEV):
        mask = onehot[m:m + 1].astype(BF16)
        gram = dot_nn(hi[...] * mask, z_ref[...]) + dot_nn(lo[...] * mask, z_ref[...])
        put_lanes(mat, slice(m * fr, (m + 1) * fr), 0, gram + eye)
    rm = resid * onehot
    rm_high = rm.astype(BF16)
    rm_low = (rm - rm_high.astype(F32)).astype(BF16)
    rhs = dot_nn(rm_high, z_ref[...]) + dot_nn(rm_low, z_ref[...])

    for k0 in range(0, fr, PANEL):
        lane0 = (k0 // 128) * 128
        orig = [get_lanes(mat, pl.ds(k0 + i, MEM_DEV, stride=fr), lane0) for i in range(PANEL)]
        wide = (MEM_DEV, 128)
        rows = [[o[:, c:c + 128] for c in range(0, o.shape[1], 128)]
                + [jnp.broadcast_to(rhs[:, k0 + i:k0 + i + 1], wide)]
                for i, o in enumerate(orig)]
        reduce_block(rows, k0 - lane0, range(BLOCK), range(BLOCK, PANEL))
        reduce_block(rows, k0 - lane0, range(BLOCK, PANEL), range(BLOCK))
        ys = [jnp.concatenate([r[-1]] * (len(r) - 1), axis=1) for r in rows]
        rows = [r[0] if len(r) == 2 else jnp.concatenate(r[:-1], axis=1) for r in rows]
        tail = rhs[:, lane0:]
        lanes = lax.broadcasted_iota(jnp.int32, tail.shape, 1) + lane0
        drop = jnp.zeros_like(tail)
        place = tail
        for i in range(PANEL):
            drop = drop + orig[i] * ys[i]
            place = jnp.where(lanes == k0 + i, ys[i], place)
        tail = jnp.where(lanes >= k0 + PANEL, tail - drop, place)
        rhs = tail if lane0 == 0 else jnp.concatenate([rhs[:, :lane0], tail], axis=1)
        for i in range(PANEL):
            put_lanes(red, slice((k0 + i) * MEM_DEV, (k0 + i + 1) * MEM_DEV), lane0, rows[i])
        top = k0 + PANEL
        if top < fr:
            lane1 = (top // 128) * 128
            row1 = lane1
            for m in range(MEM_DEV):
                o = get_lanes(mat, slice(m * fr + k0, m * fr + k0 + PANEL), row1)
                w = get_lanes(red, pl.ds(k0 * MEM_DEV + m, PANEL, stride=MEM_DEV), lane1)
                o1, o2, o3 = three_parts(o)
                w1, w2, w3 = three_parts(w)
                left = jnp.concatenate([o1, o1, o2, o2, o1, o3], axis=0)
                right = jnp.concatenate([w1, w2, w1, w2, w3, w1], axis=0)
                rest = slice(m * fr + row1, (m + 1) * fr)
                put_lanes(mat, rest, lane1, get_lanes(mat, rest, lane1) - dot_tn(left, right))

    lanes = lax.broadcasted_iota(jnp.int32, rhs.shape, 1)
    sol = jnp.where(lanes >= fr - PANEL, rhs, 0.0)
    for k0 in range(fr - 2 * PANEL, -1, -PANEL):
        new = sol
        lane0 = (k0 // 128) * 128
        for i in range(PANEL):
            w = get_lanes(red, slice((k0 + i) * MEM_DEV, (k0 + i + 1) * MEM_DEV), lane0)
            d = jnp.sum(w * sol[:, lane0:], axis=1, keepdims=True)
            new = jnp.where(lanes == k0 + i, rhs - d, new)
        sol = new
    coef = -sol
    coef_ref[...] = coef
    chigh = coef.astype(BF16)
    clow = (coef - chigh.astype(F32)).astype(BF16)
    scores = dot_nn(chigh, zt[...]) + dot_nn(clow, zt[...])
    back = jnp.sum(scores * onehot, axis=0, keepdims=True)
    for o in range(owners):
        back_ref[o] = back[:, o * cap:(o + 1) * cap]


def unpack_kernel(back_ref, slot_ref, out_ref):
    owners, _, cap = back_ref.shape
    back = back_ref[:, 0, :]
    hot_owner, hot_cap = owner_hot(slot_ref[...], owners, cap)
    rows = dot_tn(back, hot_owner, HIGH)
    out_ref[...] = jnp.sum(rows * hot_cap, axis=0, keepdims=True)


VMEM_LIMIT = 32 * 1024 * 1024
STAGE_LIMIT = 20 * 1024 * 1024


def on_chip(kernel, name, outs, *ins):
    vmem = pl.BlockSpec(memory_space=pltpu.VMEM)
    return pl.pallas_call(
        kernel,
        in_specs=[vmem] * len(ins),
        out_specs=[vmem] * len(outs),
        out_shape=[jax.ShapeDtypeStruct(s, d) for s, d in outs],
        compiler_params=pltpu.CompilerParams(vmem_limit_bytes=STAGE_LIMIT),
        name=name,
    )(*ins)


PH1 = ("core", "z")
PH2 = ("x", "y")


def on_device(features, re_features, member_id, slot, labels, offsets, feature_scale, w_start,
              *, sizes):
    n1 = sizes["core"] * sizes["z"]
    n2 = sizes["x"] * sizes["y"]
    n_mem = sizes["y"] * sizes["z"]
    n_grp = sizes["x"] * sizes["core"]
    rows, f = features.shape
    fr = re_features.shape[1]
    slots = 2 * rows
    cap = slots // n_mem
    slot_row = slot.reshape(1, rows)
    lab = labels.astype(F32).reshape(1, rows)
    off = offsets.reshape(1, rows)
    scale = feature_scale.reshape(1, f)
    w = w_start.reshape(1, f)
    code = (member_id % MEM_DEV + 8 * labels + 16).astype(F32).reshape(1, rows)

    def exchange(v, axes):
        return lax.all_to_all(v, axes, 0, 0, tiled=True)

    def reduce_rest(parts):
        got = exchange(parts, PH1)
        mid, = on_chip(again_kernel, "again", [((n2, 1, f), F32)], got)
        return exchange(mid, PH2)

    vmem = pl.BlockSpec(memory_space=pltpu.VMEM)
    packed = pl.pallas_call(
        z_pack_kernel,
        in_specs=[vmem, vmem],
        out_specs=pl.BlockSpec(memory_space=pltpu.HBM),
        out_shape=pltpu.HBM((slots, fr), BF16),
        scratch_shapes=[pltpu.VMEM((8, slots // 8, fr), BF16), pltpu.SemaphoreType.DMA((8,))],
        compiler_params=pltpu.CompilerParams(vmem_limit_bytes=STAGE_LIMIT),
        name="z_pack",
    )(slot_row, re_features)
    packed, scale = lax.optimization_barrier((packed, scale))
    z_got = lax.all_to_all(packed.reshape(n_mem, cap, fr), ("y", "z"), 0, 0, tiled=True)
    z_got = z_got.reshape(slots, fr)

    vec = ((1, f), F32)
    small = ((1, 128), F32)
    row = ((1, rows), F32)
    parts = ((n1, 1, f), F32)
    gpart, score, curv = on_chip(grad_first_kernel, "grad_first", [parts, row, row],
                                 features, scale, w, off, lab)
    for it in range(NEWTON):
        g2 = reduce_rest(gpart)
        hpart, p, rr, t = on_chip(cg_first_kernel, "cg_first", [parts, vec, small, row],
                                  features, g2, scale, w, curv)
        h2 = reduce_rest(hpart)
        if it == 0:
            h2, z_got = lax.optimization_barrier((h2, z_got))
        hpart, p, r, u, rr, t, m = on_chip(
            cg_next_kernel, "cg_next", [parts, vec, vec, vec, small, row, row],
            features, h2, scale, curv, p, rr, t)
        h2 = reduce_rest(hpart)
        ins = (features, h2, scale, curv, p, r, u, rr, t, m)
        if it + 1 < NEWTON:
            spart, p, u, rr, t, m = on_chip(
                cg_last_kernel, "cg_last", [((n1 * n2, 1, 128), F32), vec, vec, small, row, row],
                *ins)
            sgot = exchange(spart, ("x", "core", "y", "z"))
            gpart, w, score, curv = on_chip(
                grad_next_kernel, "grad_next", [parts, vec, row, row],
                features, sgot, rr, w, u, p, score, t, m, off, lab)
        else:
            send, p, u, rr = on_chip(
                cg_last_pack_kernel, "cg_last_pack",
                [((n_mem, 1, 4 * cap), F32), vec, vec, small],
                *ins, score, slot_row, code)
    got = exchange(send, ("y", "z"))
    part, = on_chip(part_kernel, "part", [((n_grp, 1, 128), F32)], got)
    part = exchange(part, ("x", "core"))
    z_got = pltpu.with_memory_space_constraint(z_got, pltpu.HBM)
    w, member_coef, back = pl.pallas_call(
        member_kernel,
        in_specs=[pl.BlockSpec(memory_space=pltpu.HBM)] + [vmem] * 6,
        out_shape=[jax.ShapeDtypeStruct((1, f), F32),
                   jax.ShapeDtypeStruct((MEM_DEV, fr), F32),
                   jax.ShapeDtypeStruct((n_mem, 1, cap), F32)],
        scratch_shapes=[pltpu.VMEM((1, slots), F32)] * 3
        + [pltpu.VMEM((fr, slots), BF16)] * 3
        + [pltpu.VMEM((MEM_DEV * fr, 128), F32)] * 4
        + [pltpu.VMEM((slots, fr), BF16), pltpu.SemaphoreType.DMA(())],
        compiler_params=pltpu.CompilerParams(vmem_limit_bytes=VMEM_LIMIT),
        name="members",
    )(z_got, got, part, rr, w, u, p)
    returned = exchange(back, ("y", "z"))
    row_offsets = pl.pallas_call(
        unpack_kernel,
        out_shape=jax.ShapeDtypeStruct((1, rows), F32),
        compiler_params=pltpu.CompilerParams(vmem_limit_bytes=VMEM_LIMIT),
        name="unpack",
    )(returned, slot_row)
    return (w.reshape(f), member_coef, row_offsets.reshape(rows))


def solution(mesh):
    n_grp, n_mem = mesh.shape["grp"], mesh.shape["mem"]
    shape = {"x": n_grp // 2, "core": 2, "y": 4, "z": n_mem // 4}
    fine = Mesh(mesh.devices.reshape(tuple(shape.values())), tuple(shape))
    cut = P(("x", "core", "y", "z"))
    cut2 = P(("x", "core", "y", "z"), None)
    return jax.shard_map(
        functools.partial(on_device, sizes=shape),
        mesh=fine,
        in_specs=(cut2, cut2, cut, cut, cut, cut, P(), P()),
        out_specs=(P(), cut2, cut),
        check_vma=False,
    )
```

```python
import functools
import jax
import jax.numpy as jnp
from jax import lax
from jax.experimental import pallas as pl
from jax.experimental.pallas import tpu as pltpu
from jax.sharding import Mesh, PartitionSpec as P

MEM_DEV = 8
NEWTON = 2
RIDGE = 1.0
PANEL = 16
BLOCK = 8
STEPS = 4
F32 = jnp.float32
BF16 = jnp.bfloat16
HIGH = lax.Precision.HIGHEST


def dot_nn(a, b, precision=None):
    return lax.dot_general(a, b, (((1,), (0,)), ((), ())), precision=precision,
                           preferred_element_type=F32)


def dot_nt(a, b, precision=None):
    return lax.dot_general(a, b, (((1,), (1,)), ((), ())), precision=precision,
                           preferred_element_type=F32)


def dot_tn(a, b, precision=None):
    return lax.dot_general(a, b, (((0,), (0,)), ((), ())), precision=precision,
                           preferred_element_type=F32)


def split_rows(row):
    high = row.astype(BF16).astype(F32)
    low = row - high
    at = lax.broadcasted_iota(jnp.int32, (8, row.shape[1]), 0)
    return jnp.where(at == 0, high, jnp.where(at == 1, low, 0.0)).astype(BF16)


def sigmoid(x):
    return 1.0 / (1.0 + jnp.exp(-x))


def total(row):
    return jnp.sum(row, axis=1, keepdims=True)


def sum_parts(ref):
    acc = ref[0]
    for i in range(1, ref.shape[0]):
        acc = acc + ref[i]
    return acc


def forward(xs, x_ref, xs_ref, row_ref, arrive=None):
    xs_ref[...] = xs
    block = x_ref.shape[0] // STEPS

    def body(i, carry):
        at = pl.multiple_of(i * block, block)
        if arrive is not None:
            arrive(i, at, block)
        both = dot_nt(xs_ref[...], x_ref[pl.ds(at, block), :])
        row_ref[:, pl.ds(at, block)] = both[0:1] + both[1:2]
        return carry

    lax.fori_loop(0, STEPS, body, 0)
    return row_ref[...]


def backward(row, x_ref, split_ref, out_ref):
    split_ref[...] = split_rows(row)
    block = x_ref.shape[1] // STEPS

    def body(i, carry):
        at = pl.multiple_of(i * block, block)
        both = dot_nn(split_ref[...], x_ref[:, pl.ds(at, block)])
        val = both[0:1] + both[1:2]
        for j in range(out_ref.shape[0]):
            out_ref[j, :, pl.ds(at, block)] = val
        return carry

    lax.fori_loop(0, STEPS, body, 0)


def start_kernel(x_hbm, z_hbm, slot_hbm, member_hbm, lab_hbm, off_hbm, scale_hbm, w_hbm,
                 packed_ref, x_ref, slot_ref, code_ref, lab_ref, off_ref, scale_ref, w_ref,
                 out_ref, score_ref, curv_ref,
                 z_ref, member_ref, int_ref, buf, xs_ref, split_ref, sems, xsems, psems):
    pairs = [(slot_hbm, slot_ref), (z_hbm, z_ref), (scale_hbm, scale_ref), (w_hbm, w_ref),
             (member_hbm, member_ref), (lab_hbm, int_ref), (off_hbm, off_ref)]
    loads = [pltpu.make_async_copy(src, dst, sems.at[i]) for i, (src, dst) in enumerate(pairs)]
    for load in loads:
        load.start()

    def chunk(i, at, block):
        return pltpu.make_async_copy(x_hbm.at[pl.ds(at, block)], x_ref.at[pl.ds(at, block)],
                                     xsems.at[i])

    block = x_ref.shape[0] // STEPS
    for i in range(STEPS):
        chunk(i, i * block, block).start()
    loads[0].wait()
    loads[1].wait()
    size = buf.shape[1]
    stores = []
    for b in range(buf.shape[0]):
        rows = lax.broadcasted_iota(jnp.int32, (size, slot_ref.shape[1]), 0) + b * size
        hot = jnp.where(rows == slot_ref[...], 1.0, 0.0).astype(BF16)
        buf[b] = dot_nn(hot, z_ref[...]).astype(BF16)
        stores.append(pltpu.make_async_copy(
            buf.at[b], packed_ref.at[pl.ds(b * size, size)], psems.at[b]))
        stores[-1].start()
    for load in loads[2:]:
        load.wait()
    labels = int_ref[...]
    lab_ref[...] = labels.astype(F32)
    code_ref[...] = (member_ref[...] % MEM_DEV + 8 * labels + 16).astype(F32)
    score = forward(split_rows(scale_ref[...] * w_ref[...]), x_ref, xs_ref, score_ref,
                    lambda i, at, size: chunk(i, at, size).wait())
    prob = sigmoid(score + off_ref[...])
    curv_ref[...] = prob * (1.0 - prob)
    backward(prob - lab_ref[...], x_ref, split_ref, out_ref)
    for store in stores:
        store.wait()


def grad_next_kernel(x_ref, part_ref, rr_ref, w_ref, u_ref, p_ref, score_ref, t_ref, m_ref,
                     off_ref, lab_ref, out_ref, w_out, score_out, curv_ref, xs_ref, split_ref):
    a = last_coef(part_ref, rr_ref, p_ref)
    w_out[...] = w_ref[...] + (u_ref[...] + a * p_ref[...])
    score = score_ref[...] + (m_ref[...] + a * t_ref[...])
    prob = sigmoid(score + off_ref[...])
    score_out[...] = score
    curv_ref[...] = prob * (1.0 - prob)
    backward(prob - lab_ref[...], x_ref, split_ref, out_ref)


def last_coef(part_ref, rr_ref, p_ref):
    p = p_ref[...]
    php = jnp.sum(part_ref[:, 0, :], axis=0, keepdims=True)[:, 0:1] + RIDGE * total(p * p)
    return rr_ref[:, 0:1] / php


def cg_first_kernel(x_ref, sum_ref, scale_ref, w_ref, curv_ref, out_ref, p_out, rr_out, t_ref,
                    xs_ref, split_ref):
    r = -(scale_ref[...] * sum_parts(sum_ref) + RIDGE * w_ref[...])
    p_out[...] = r
    rr_out[...] = jnp.broadcast_to(total(r * r), rr_out.shape)
    t = forward(split_rows(scale_ref[...] * r), x_ref, xs_ref, t_ref)
    backward(curv_ref[...] * t, x_ref, split_ref, out_ref)


def cg_update(sum_ref, scale_ref, p_ref, r_ref, u_ref, rr_ref, p_out, r_out, u_out, rr_out):
    p = p_ref[...]
    q = scale_ref[...] * sum_parts(sum_ref) + RIDGE * p
    rr = rr_ref[:, 0:1]
    a = rr / total(p * q)
    u = a * p if u_ref is None else u_ref[...] + a * p
    r = r_ref[...] - a * q
    nn = total(r * r)
    p = r + (nn / rr) * p
    u_out[...] = u
    if r_out is not None:
        r_out[...] = r
    p_out[...] = p
    rr_out[...] = jnp.broadcast_to(nn, rr_out.shape)
    return a, split_rows(scale_ref[...] * p)


def cg_next_kernel(x_ref, sum_ref, scale_ref, curv_ref, p_ref, rr_ref, t_in,
                   out_ref, p_out, r_out, u_out, rr_out, t_ref, m_ref, xs_ref, split_ref):
    a, xs = cg_update(sum_ref, scale_ref, p_ref, p_ref, None, rr_ref, p_out, r_out, u_out, rr_out)
    m_ref[...] = a * t_in[...]
    t = forward(xs, x_ref, xs_ref, t_ref)
    backward(curv_ref[...] * t, x_ref, split_ref, out_ref)


def cg_last_kernel(x_ref, sum_ref, scale_ref, curv_ref, p_ref, r_ref, u_ref, rr_ref, t_in, m_in,
                   out_ref, p_out, u_out, rr_out, t_ref, m_ref, xs_ref, split_ref):
    a, xs = cg_update(sum_ref, scale_ref, p_ref, r_ref, u_ref, rr_ref, p_out, None, u_out, rr_out)
    m_ref[...] = m_in[...] + a * t_in[...]
    t = forward(xs, x_ref, xs_ref, t_ref)
    out_ref[...] = jnp.broadcast_to(total(curv_ref[...] * t * t).reshape(1, 1, 1), out_ref.shape)


def owner_hot(slot, owners, cap):
    rows = lax.broadcasted_iota(jnp.int32, (owners, slot.shape[1]), 0)
    hot_owner = jnp.where(rows == slot // cap, 1.0, 0.0)
    lanes = lax.broadcasted_iota(jnp.int32, (cap, slot.shape[1]), 0)
    hot_cap = jnp.where(lanes == slot % cap, 1.0, 0.0)
    return hot_owner, hot_cap


def cg_last_pack_kernel(x_ref, sum_ref, scale_ref, curv_ref, p_ref, r_ref, u_ref, rr_ref, t_in,
                        m_in, score_ref, slot_ref, code_ref, out_ref, p_out, u_out, rr_out,
                        t_ref, xs_ref, split_ref):
    a, xs = cg_update(sum_ref, scale_ref, p_ref, r_ref, u_ref, rr_ref, p_out, None, u_out, rr_out)
    owners, cap = out_ref.shape[0], out_ref.shape[2] // 4
    hot_owner, hot_cap = owner_hot(slot_ref[...], owners, cap)
    t = forward(xs, x_ref, xs_ref, t_ref)
    done = score_ref[...] + (m_in[...] + a * t_in[...])
    php = total(curv_ref[...] * t * t)
    left = jnp.concatenate([hot_owner * done, hot_owner * t, hot_owner * code_ref[...]], axis=0)
    send = dot_nt(left, hot_cap, HIGH)
    part = jnp.broadcast_to(php, (1, cap))
    for i in range(owners):
        out_ref[i] = jnp.concatenate(
            [send[j * owners + i:j * owners + i + 1] for j in range(3)] + [part], axis=1)


def again_kernel(sum_ref, out_ref):
    val = sum_parts(sum_ref)
    for i in range(out_ref.shape[0]):
        out_ref[i] = val


def part_kernel(arr_ref, out_ref):
    last = arr_ref.shape[2] - 1
    got = arr_ref[:, 0, :]
    val = jnp.sum(got, axis=0, keepdims=True)[:, last:]
    out_ref[...] = jnp.broadcast_to(val.reshape(1, 1, 1), out_ref.shape)


def three_parts(v):
    a = v.astype(BF16)
    rest = v - a.astype(F32)
    b = rest.astype(BF16)
    c = (rest - b.astype(F32)).astype(BF16)
    return a, b, c


def get_lanes(halves, rows, lane):
    if lane:
        return halves[1][rows, :]
    return jnp.concatenate([halves[0][rows, :], halves[1][rows, :]], axis=1)


def put_lanes(halves, rows, lane, value):
    if lane:
        halves[1][rows, :] = value
    else:
        halves[0][rows, :] = value[:, :128]
        halves[1][rows, :] = value[:, 128:]


def reduce_block(rows, lane, block, others):
    def at(i, j):
        return jnp.broadcast_to(rows[i][0][:, lane + j:lane + j + 1], rows[i][0].shape)

    block, others = list(block), list(others)
    c = {(i, j): at(i, j) for i in block for j in block if j <= i}
    far = {(i, j): at(i, j) for i in others for j in block}
    lower, inv = {}, {}
    for j in block:
        inv[j] = 1.0 / c[j, j]
        for i in block:
            if i > j:
                lower[i, j] = c[i, j] * inv[j]
        for i in block:
            for k in block:
                if j < k <= i:
                    c[i, k] = c[i, k] - lower[i, j] * c[k, j]
    for j in block:
        for i in block:
            if i > j:
                rows[i] = [v - lower[i, j] * w for v, w in zip(rows[i], rows[j])]
    for j in block:
        rows[j] = [w * inv[j] for w in rows[j]]
    for j in reversed(block):
        for i in block:
            if i < j:
                rows[i] = [v - lower[j, i] * w for v, w in zip(rows[i], rows[j])]
    for j in block:
        for i in others:
            rows[i] = [v - far[i, j] * w for v, w in zip(rows[i], rows[j])]


def member_kernel(z_hbm, arr_ref, part_ref, rr_ref, w_ref, u_ref, p_ref,
                  w_out, coef_ref, back_ref,
                  base, tvec, code, zt, hi, lo, mat0, mat1, red0, red1, z_ref, sem):
    copy = pltpu.make_async_copy(z_hbm, z_ref, sem)
    copy.start()
    owners = arr_ref.shape[0]
    cap = arr_ref.shape[2] // 4
    fr = z_ref.shape[1]
    slots = z_ref.shape[0]
    p = p_ref[...]
    php = jnp.sum(part_ref[:, 0, :], axis=0, keepdims=True)[:, 0:1] + RIDGE * total(p * p)
    a = rr_ref[:, 0:1] / php
    w_out[...] = w_ref[...] + (u_ref[...] + a * p)
    for o in range(owners):
        got = arr_ref[o]
        base[:, o * cap:(o + 1) * cap] = got[:, 0:cap]
        tvec[:, o * cap:(o + 1) * cap] = got[:, cap:2 * cap]
        code[:, o * cap:(o + 1) * cap] = got[:, 2 * cap:3 * cap]
    prob = sigmoid(base[...] + a * tvec[...])
    curv = prob * (1.0 - prob)
    codes = code[...]
    label = jnp.where(codes >= 24.0, 1.0, 0.0)
    resid = prob - label
    local = codes - 16.0 - 8.0 * label
    at = lax.broadcasted_iota(jnp.int32, (MEM_DEV, slots), 0).astype(F32)
    onehot = jnp.where(local == at, 1.0, 0.0)

    copy.wait()
    z_t = z_ref[...].T
    zt[...] = z_t
    chunk = 512
    for c in range(0, slots, chunk):
        cz = zt[:, c:c + chunk].astype(F32) * curv[:, c:c + chunk]
        high = cz.astype(BF16)
        hi[:, c:c + chunk] = high
        lo[:, c:c + chunk] = (cz - high.astype(F32)).astype(BF16)
    mat, red = (mat0, mat1), (red0, red1)
    eye = jnp.where(lax.broadcasted_iota(jnp.int32, (fr, fr), 0)
                    == lax.broadcasted_iota(jnp.int32, (fr, fr), 1), RIDGE, 0.0)
    for m in range(MEM_DEV):
        mask = onehot[m:m + 1].astype(BF16)
        gram = dot_nn(hi[...] * mask, z_ref[...]) + dot_nn(lo[...] * mask, z_ref[...])
        put_lanes(mat, slice(m * fr, (m + 1) * fr), 0, gram + eye)
    rm = resid * onehot
    rm_high = rm.astype(BF16)
    rm_low = (rm - rm_high.astype(F32)).astype(BF16)
    rhs = dot_nn(rm_high, z_ref[...]) + dot_nn(rm_low, z_ref[...])

    for k0 in range(0, fr, PANEL):
        lane0 = (k0 // 128) * 128
        orig = [get_lanes(mat, pl.ds(k0 + i, MEM_DEV, stride=fr), lane0) for i in range(PANEL)]
        wide = (MEM_DEV, 128)
        rows = [[o[:, c:c + 128] for c in range(0, o.shape[1], 128)]
                + [jnp.broadcast_to(rhs[:, k0 + i:k0 + i + 1], wide)]
                for i, o in enumerate(orig)]
        reduce_block(rows, k0 - lane0, range(BLOCK), range(BLOCK, PANEL))
        reduce_block(rows, k0 - lane0, range(BLOCK, PANEL), range(BLOCK))
        ys = [jnp.concatenate([r[-1]] * (len(r) - 1), axis=1) for r in rows]
        rows = [r[0] if len(r) == 2 else jnp.concatenate(r[:-1], axis=1) for r in rows]
        tail = rhs[:, lane0:]
        lanes = lax.broadcasted_iota(jnp.int32, tail.shape, 1) + lane0
        drop = jnp.zeros_like(tail)
        place = tail
        for i in range(PANEL):
            drop = drop + orig[i] * ys[i]
            place = jnp.where(lanes == k0 + i, ys[i], place)
        tail = jnp.where(lanes >= k0 + PANEL, tail - drop, place)
        rhs = tail if lane0 == 0 else jnp.concatenate([rhs[:, :lane0], tail], axis=1)
        for i in range(PANEL):
            put_lanes(red, slice((k0 + i) * MEM_DEV, (k0 + i + 1) * MEM_DEV), lane0, rows[i])
        top = k0 + PANEL
        if top < fr:
            lane1 = (top // 128) * 128
            row1 = lane1
            for m in range(MEM_DEV):
                o = get_lanes(mat, slice(m * fr + k0, m * fr + k0 + PANEL), row1)
                w = get_lanes(red, pl.ds(k0 * MEM_DEV + m, PANEL, stride=MEM_DEV), lane1)
                o1, o2, o3 = three_parts(o)
                w1, w2, w3 = three_parts(w)
                left = jnp.concatenate([o1, o1, o2, o2, o1, o3], axis=0)
                right = jnp.concatenate([w1, w2, w1, w2, w3, w1], axis=0)
                rest = slice(m * fr + row1, (m + 1) * fr)
                put_lanes(mat, rest, lane1, get_lanes(mat, rest, lane1) - dot_tn(left, right))

    lanes = lax.broadcasted_iota(jnp.int32, rhs.shape, 1)
    sol = jnp.where(lanes >= fr - PANEL, rhs, 0.0)
    for k0 in range(fr - 2 * PANEL, -1, -PANEL):
        new = sol
        lane0 = (k0 // 128) * 128
        for i in range(PANEL):
            w = get_lanes(red, slice((k0 + i) * MEM_DEV, (k0 + i + 1) * MEM_DEV), lane0)
            d = jnp.sum(w * sol[:, lane0:], axis=1, keepdims=True)
            new = jnp.where(lanes == k0 + i, rhs - d, new)
        sol = new
    coef = -sol
    coef_ref[...] = coef
    chigh = coef.astype(BF16)
    clow = (coef - chigh.astype(F32)).astype(BF16)
    scores = dot_nn(chigh, zt[...]) + dot_nn(clow, zt[...])
    back = jnp.sum(scores * onehot, axis=0, keepdims=True)
    for o in range(owners):
        back_ref[o] = back[:, o * cap:(o + 1) * cap]


def unpack_kernel(back_ref, slot_ref, out_ref):
    owners, _, cap = back_ref.shape
    back = back_ref[:, 0, :]
    hot_owner, hot_cap = owner_hot(slot_ref[...], owners, cap)
    rows = dot_tn(back, hot_owner, HIGH)
    out_ref[...] = jnp.sum(rows * hot_cap, axis=0, keepdims=True)


VMEM_LIMIT = 32 * 1024 * 1024
STAGE_LIMIT = 20 * 1024 * 1024


def on_chip(kernel, name, outs, *ins, scratch=()):
    vmem = pl.BlockSpec(memory_space=pltpu.VMEM)
    return pl.pallas_call(
        kernel,
        in_specs=[vmem] * len(ins),
        out_specs=[vmem] * len(outs),
        out_shape=[jax.ShapeDtypeStruct(s, d) for s, d in outs],
        scratch_shapes=list(scratch),
        compiler_params=pltpu.CompilerParams(vmem_limit_bytes=STAGE_LIMIT),
        name=name,
    )(*ins)


PH1 = ("core", "z")
PH2 = ("x", "y")


def on_device(features, re_features, member_id, slot, labels, offsets, feature_scale, w_start,
              *, sizes):
    n1 = sizes["core"] * sizes["z"]
    n2 = sizes["x"] * sizes["y"]
    n_mem = sizes["y"] * sizes["z"]
    n_grp = sizes["x"] * sizes["core"]
    rows, f = features.shape
    fr = re_features.shape[1]
    slots = 2 * rows
    cap = slots // n_mem
    def exchange(v, axes):
        return lax.all_to_all(v, axes, 0, 0, tiled=True)

    def reduce_rest(parts):
        got = exchange(parts, PH1)
        mid, = on_chip(again_kernel, "again", [((n2, 1, f), F32)], got)
        return exchange(mid, PH2)

    tmp = [pltpu.VMEM((8, f), BF16), pltpu.VMEM((8, rows), BF16)]
    vec = ((1, f), F32)
    small = ((1, 128), F32)
    row = ((1, rows), F32)
    parts = ((n1, 1, f), F32)
    vmem = pl.BlockSpec(memory_space=pltpu.VMEM)
    hbm = pl.BlockSpec(memory_space=pltpu.HBM)
    outs = [((rows, f), BF16), ((1, rows), jnp.int32), row, row, row, vec, vec, parts, row, row]
    packed, x, slot_row, code, lab, off, scale, w, gpart, score, curv = pl.pallas_call(
        start_kernel,
        in_specs=[hbm] * 8,
        out_specs=[hbm] + [vmem] * len(outs),
        out_shape=[pltpu.HBM((slots, fr), BF16)] + [jax.ShapeDtypeStruct(*o) for o in outs],
        scratch_shapes=[pltpu.VMEM((rows, fr), BF16)] + [pltpu.VMEM((1, rows), jnp.int32)] * 2
        + [pltpu.VMEM((8, slots // 8, fr), BF16)] + tmp
        + [pltpu.SemaphoreType.DMA((7,)), pltpu.SemaphoreType.DMA((STEPS,)),
           pltpu.SemaphoreType.DMA((8,))],
        compiler_params=pltpu.CompilerParams(vmem_limit_bytes=STAGE_LIMIT),
        name="start",
    )(*[pltpu.with_memory_space_constraint(v, pltpu.HBM) for v in (
        features, re_features, slot.reshape(1, rows), member_id.reshape(1, rows),
        labels.reshape(1, rows), offsets.reshape(1, rows), feature_scale.reshape(1, f),
        w_start.reshape(1, f))])
    z_got = lax.all_to_all(packed.reshape(n_mem, cap, fr), ("y", "z"), 0, 0, tiled=True)
    z_got = z_got.reshape(slots, fr)
    for it in range(NEWTON):
        g2 = reduce_rest(gpart)
        hpart, p, rr, t = on_chip(cg_first_kernel, "cg_first", [parts, vec, small, row],
                                  x, g2, scale, w, curv, scratch=tmp)
        h2 = reduce_rest(hpart)
        if it == 0:
            h2, z_got = lax.optimization_barrier((h2, z_got))
        hpart, p, r, u, rr, t, m = on_chip(
            cg_next_kernel, "cg_next", [parts, vec, vec, vec, small, row, row],
            x, h2, scale, curv, p, rr, t, scratch=tmp)
        h2 = reduce_rest(hpart)
        ins = (x, h2, scale, curv, p, r, u, rr, t, m)
        if it + 1 < NEWTON:
            spart, p, u, rr, t, m = on_chip(
                cg_last_kernel, "cg_last", [((n1 * n2, 1, 128), F32), vec, vec, small, row, row],
                *ins, scratch=tmp)
            sgot = exchange(spart, ("x", "core", "y", "z"))
            gpart, w, score, curv = on_chip(
                grad_next_kernel, "grad_next", [parts, vec, row, row],
                x, sgot, rr, w, u, p, score, t, m, off, lab, scratch=tmp)
        else:
            send, p, u, rr = on_chip(
                cg_last_pack_kernel, "cg_last_pack",
                [((n_mem, 1, 4 * cap), F32), vec, vec, small],
                *ins, score, slot_row, code, scratch=[pltpu.VMEM((1, rows), F32)] + tmp)
    got = exchange(send, ("y", "z"))
    part, = on_chip(part_kernel, "part", [((n_grp, 1, 128), F32)], got)
    part = exchange(part, ("x", "core"))
    z_got = pltpu.with_memory_space_constraint(z_got, pltpu.HBM)
    w, member_coef, back = pl.pallas_call(
        member_kernel,
        in_specs=[pl.BlockSpec(memory_space=pltpu.HBM)] + [vmem] * 6,
        out_shape=[jax.ShapeDtypeStruct((1, f), F32),
                   jax.ShapeDtypeStruct((MEM_DEV, fr), F32),
                   jax.ShapeDtypeStruct((n_mem, 1, cap), F32)],
        scratch_shapes=[pltpu.VMEM((1, slots), F32)] * 3
        + [pltpu.VMEM((fr, slots), BF16)] * 3
        + [pltpu.VMEM((MEM_DEV * fr, 128), F32)] * 4
        + [pltpu.VMEM((slots, fr), BF16), pltpu.SemaphoreType.DMA(())],
        compiler_params=pltpu.CompilerParams(vmem_limit_bytes=VMEM_LIMIT),
        name="members",
    )(z_got, got, part, rr, w, u, p)
    returned = exchange(back, ("y", "z"))
    row_offsets = pl.pallas_call(
        unpack_kernel,
        out_shape=jax.ShapeDtypeStruct((1, rows), F32),
        compiler_params=pltpu.CompilerParams(vmem_limit_bytes=VMEM_LIMIT),
        name="unpack",
    )(returned, slot_row)
    return (w.reshape(f), member_coef, row_offsets.reshape(rows))


def solution(mesh):
    n_grp, n_mem = mesh.shape["grp"], mesh.shape["mem"]
    shape = {"x": n_grp // 2, "core": 2, "y": 4, "z": n_mem // 4}
    fine = Mesh(mesh.devices.reshape(tuple(shape.values())), tuple(shape))
    cut = P(("x", "core", "y", "z"))
    cut2 = P(("x", "core", "y", "z"), None)
    return jax.shard_map(
        functools.partial(on_device, sizes=shape),
        mesh=fine,
        in_specs=(cut2, cut2, cut, cut, cut, cut, P(), P()),
        out_specs=(P(), cut2, cut),
        check_vma=False,
    )
```

```python
import functools
import jax
import jax.numpy as jnp
from jax import lax
from jax.experimental import pallas as pl
from jax.experimental.pallas import tpu as pltpu
from jax.sharding import Mesh, PartitionSpec as P

MEM_DEV = 8
NEWTON = 2
RIDGE = 1.0
PANEL = 16
BLOCK = 8
STEPS = 4
UNROLL = 4
GRAM_UNROLL = 1
F32 = jnp.float32
BF16 = jnp.bfloat16
HIGH = lax.Precision.HIGHEST


def dot_nn(a, b, precision=None):
    return lax.dot_general(a, b, (((1,), (0,)), ((), ())), precision=precision,
                           preferred_element_type=F32)


def dot_nt(a, b, precision=None):
    return lax.dot_general(a, b, (((1,), (1,)), ((), ())), precision=precision,
                           preferred_element_type=F32)


def dot_tn(a, b, precision=None):
    return lax.dot_general(a, b, (((0,), (0,)), ((), ())), precision=precision,
                           preferred_element_type=F32)


def split_rows(row):
    high = row.astype(BF16).astype(F32)
    low = row - high
    at = lax.broadcasted_iota(jnp.int32, (8, row.shape[1]), 0)
    return jnp.where(at == 0, high, jnp.where(at == 1, low, 0.0)).astype(BF16)


def sigmoid(x):
    return 1.0 / (1.0 + jnp.exp(-x))


def total(row):
    return jnp.sum(row, axis=1, keepdims=True)


def sum_parts(ref):
    acc = ref[0]
    for i in range(1, ref.shape[0]):
        acc = acc + ref[i]
    return acc


def forward(xs, x_ref, xs_ref, row_ref, arrive=None):
    xs_ref[...] = xs
    block = x_ref.shape[0] // STEPS

    def body(i, carry):
        at = pl.multiple_of(i * block, block)
        if arrive is not None:
            arrive(i, at, block)
        both = dot_nt(xs_ref[...], x_ref[pl.ds(at, block), :])
        row_ref[:, pl.ds(at, block)] = both[0:1] + both[1:2]
        return carry

    lax.fori_loop(0, STEPS, body, 0)
    return row_ref[...]


def backward(row, x_ref, split_ref, out_ref):
    split_ref[...] = split_rows(row)
    block = x_ref.shape[1] // STEPS

    def body(i, carry):
        at = pl.multiple_of(i * block, block)
        both = dot_nn(split_ref[...], x_ref[:, pl.ds(at, block)])
        val = both[0:1] + both[1:2]
        for j in range(out_ref.shape[0]):
            out_ref[j, :, pl.ds(at, block)] = val
        return carry

    lax.fori_loop(0, STEPS, body, 0)


def start_kernel(x_hbm, z_hbm, slot_hbm, member_hbm, lab_hbm, off_hbm, scale_hbm, w_hbm,
                 packed_ref, slot_ref, code_ref, lab_ref, off_ref, scale_ref, w_ref,
                 out_ref, score_ref, curv_ref,
                 x_ref, z_ref, member_ref, int_ref, buf, xs_ref, split_ref, sems, xsems, psems):
    pairs = [(slot_hbm, slot_ref), (z_hbm, z_ref), (scale_hbm, scale_ref), (w_hbm, w_ref),
             (member_hbm, member_ref), (lab_hbm, int_ref), (off_hbm, off_ref)]
    loads = [pltpu.make_async_copy(src, dst, sems.at[i]) for i, (src, dst) in enumerate(pairs)]
    for load in loads:
        load.start()

    def chunk(i, at, block):
        return pltpu.make_async_copy(x_hbm.at[pl.ds(at, block)], x_ref.at[pl.ds(at, block)],
                                     xsems.at[i])

    block = x_ref.shape[0] // STEPS
    for i in range(STEPS):
        chunk(i, i * block, block).start()
    loads[0].wait()
    loads[1].wait()
    size = buf.shape[1]
    stores = []
    for b in range(buf.shape[0]):
        rows = lax.broadcasted_iota(jnp.int32, (size, slot_ref.shape[1]), 0) + b * size
        hot = jnp.where(rows == slot_ref[...], 1.0, 0.0).astype(BF16)
        buf[b] = dot_nn(hot, z_ref[...]).astype(BF16)
        stores.append(pltpu.make_async_copy(
            buf.at[b], packed_ref.at[pl.ds(b * size, size)], psems.at[b]))
        stores[-1].start()
    for load in loads[2:]:
        load.wait()
    labels = int_ref[...]
    lab_ref[...] = labels.astype(F32)
    code_ref[...] = (member_ref[...] % MEM_DEV + 8 * labels + 16).astype(F32)
    score = forward(split_rows(scale_ref[...] * w_ref[...]), x_ref, xs_ref, score_ref,
                    lambda i, at, size: chunk(i, at, size).wait())
    prob = sigmoid(score + off_ref[...])
    curv_ref[...] = prob * (1.0 - prob)
    backward(prob - lab_ref[...], x_ref, split_ref, out_ref)
    for store in stores:
        store.wait()


def grad_next_kernel(x_ref, part_ref, rr_ref, w_ref, u_ref, p_ref, score_ref, t_ref, m_ref,
                     off_ref, lab_ref, out_ref, w_out, score_out, curv_ref, xs_ref, split_ref):
    a = last_coef(part_ref, rr_ref, p_ref)
    w_out[...] = w_ref[...] + (u_ref[...] + a * p_ref[...])
    score = score_ref[...] + (m_ref[...] + a * t_ref[...])
    prob = sigmoid(score + off_ref[...])
    score_out[...] = score
    curv_ref[...] = prob * (1.0 - prob)
    backward(prob - lab_ref[...], x_ref, split_ref, out_ref)


def last_coef(part_ref, rr_ref, p_ref):
    p = p_ref[...]
    php = jnp.sum(part_ref[:, 0, :], axis=0, keepdims=True)[:, 0:1] + RIDGE * total(p * p)
    return rr_ref[:, 0:1] / php


def cg_first_kernel(x_ref, sum_ref, scale_ref, w_ref, curv_ref, out_ref, p_out, rr_out, t_ref,
                    xs_ref, split_ref, arrive=None):
    r = -(scale_ref[...] * sum_parts(sum_ref) + RIDGE * w_ref[...])
    p_out[...] = r
    rr_out[...] = jnp.broadcast_to(total(r * r), rr_out.shape)
    t = forward(split_rows(scale_ref[...] * r), x_ref, xs_ref, t_ref, arrive)
    backward(curv_ref[...] * t, x_ref, split_ref, out_ref)


def cg_load_kernel(x_hbm, sum_ref, scale_ref, w_ref, curv_ref, x_ref, out_ref, p_out, rr_out,
                   t_ref, xs_ref, split_ref, sems):
    def chunk(i, at, block):
        return pltpu.make_async_copy(x_hbm.at[pl.ds(at, block)], x_ref.at[pl.ds(at, block)],
                                     sems.at[i])

    block = x_ref.shape[0] // STEPS
    for i in range(STEPS):
        chunk(i, i * block, block).start()
    cg_first_kernel(x_ref, sum_ref, scale_ref, w_ref, curv_ref, out_ref, p_out, rr_out, t_ref,
                    xs_ref, split_ref, lambda i, at, size: chunk(i, at, size).wait())


def cg_update(sum_ref, scale_ref, p_ref, r_ref, u_ref, rr_ref, p_out, r_out, u_out, rr_out):
    p = p_ref[...]
    q = scale_ref[...] * sum_parts(sum_ref) + RIDGE * p
    rr = rr_ref[:, 0:1]
    a = rr / total(p * q)
    u = a * p if u_ref is None else u_ref[...] + a * p
    r = r_ref[...] - a * q
    nn = total(r * r)
    p = r + (nn / rr) * p
    u_out[...] = u
    if r_out is not None:
        r_out[...] = r
    p_out[...] = p
    rr_out[...] = jnp.broadcast_to(nn, rr_out.shape)
    return a, split_rows(scale_ref[...] * p)


def cg_next_kernel(x_ref, sum_ref, scale_ref, curv_ref, p_ref, rr_ref, t_in,
                   out_ref, p_out, r_out, u_out, rr_out, t_ref, m_ref, xs_ref, split_ref):
    a, xs = cg_update(sum_ref, scale_ref, p_ref, p_ref, None, rr_ref, p_out, r_out, u_out, rr_out)
    m_ref[...] = a * t_in[...]
    t = forward(xs, x_ref, xs_ref, t_ref)
    backward(curv_ref[...] * t, x_ref, split_ref, out_ref)


def cg_last_kernel(x_ref, sum_ref, scale_ref, curv_ref, p_ref, r_ref, u_ref, rr_ref, t_in, m_in,
                   out_ref, p_out, u_out, rr_out, t_ref, m_ref, xs_ref, split_ref):
    a, xs = cg_update(sum_ref, scale_ref, p_ref, r_ref, u_ref, rr_ref, p_out, None, u_out, rr_out)
    m_ref[...] = m_in[...] + a * t_in[...]
    t = forward(xs, x_ref, xs_ref, t_ref)
    out_ref[...] = jnp.broadcast_to(total(curv_ref[...] * t * t).reshape(1, 1, 1), out_ref.shape)


def owner_hot(slot, owners, cap):
    rows = lax.broadcasted_iota(jnp.int32, (owners, slot.shape[1]), 0)
    hot_owner = jnp.where(rows == slot // cap, 1.0, 0.0)
    lanes = lax.broadcasted_iota(jnp.int32, (cap, slot.shape[1]), 0)
    hot_cap = jnp.where(lanes == slot % cap, 1.0, 0.0)
    return hot_owner, hot_cap


def cg_last_pack_kernel(x_ref, sum_ref, scale_ref, curv_ref, p_ref, r_ref, u_ref, rr_ref, t_in,
                        m_in, score_ref, slot_ref, code_ref, out_ref, p_out, u_out, rr_out,
                        t_ref, xs_ref, split_ref):
    a, xs = cg_update(sum_ref, scale_ref, p_ref, r_ref, u_ref, rr_ref, p_out, None, u_out, rr_out)
    owners, cap = out_ref.shape[0], out_ref.shape[2] // 4
    hot_owner, hot_cap = owner_hot(slot_ref[...], owners, cap)
    t = forward(xs, x_ref, xs_ref, t_ref)
    done = score_ref[...] + (m_in[...] + a * t_in[...])
    php = total(curv_ref[...] * t * t)
    left = jnp.concatenate([hot_owner * done, hot_owner * t, hot_owner * code_ref[...]], axis=0)
    send = dot_nt(left, hot_cap, HIGH)
    part = jnp.broadcast_to(php, (1, cap))
    for i in range(owners):
        out_ref[i] = jnp.concatenate(
            [send[j * owners + i:j * owners + i + 1] for j in range(3)] + [part], axis=1)


def again_kernel(sum_ref, out_ref):
    val = sum_parts(sum_ref)
    for i in range(out_ref.shape[0]):
        out_ref[i] = val


def add_four_kernel(a_ref, b_ref, c_ref, d_ref, out_ref):
    out_ref[...] = (a_ref[...] + b_ref[...]) + (c_ref[...] + d_ref[...])


def part_kernel(arr_ref, out_ref):
    last = arr_ref.shape[2] - 1
    got = arr_ref[:, 0, :]
    val = jnp.sum(got, axis=0, keepdims=True)[:, last:]
    out_ref[...] = jnp.broadcast_to(val.reshape(1, 1, 1), out_ref.shape)


def three_parts(v):
    a = v.astype(BF16)
    rest = v - a.astype(F32)
    b = rest.astype(BF16)
    c = (rest - b.astype(F32)).astype(BF16)
    return a, b, c


def get_lanes(halves, rows, lane):
    if lane:
        return halves[1][rows, :]
    return jnp.concatenate([halves[0][rows, :], halves[1][rows, :]], axis=1)


def put_lanes(halves, rows, lane, value):
    if lane:
        halves[1][rows, :] = value
    else:
        halves[0][rows, :] = value[:, :128]
        halves[1][rows, :] = value[:, 128:]


def reduce_block(rows, lane, block, others):
    def at(i, j):
        return jnp.broadcast_to(rows[i][0][:, lane + j:lane + j + 1], rows[i][0].shape)

    block, others = list(block), list(others)
    c = {(i, j): at(i, j) for i in block for j in block if j <= i}
    far = {(i, j): at(i, j) for i in others for j in block}
    lower, inv = {}, {}
    for j in block:
        inv[j] = 1.0 / c[j, j]
        for i in block:
            if i > j:
                lower[i, j] = c[i, j] * inv[j]
        for i in block:
            for k in block:
                if j < k <= i:
                    c[i, k] = c[i, k] - lower[i, j] * c[k, j]
    for j in block:
        for i in block:
            if i > j:
                rows[i] = [v - lower[i, j] * w for v, w in zip(rows[i], rows[j])]
    for j in block:
        rows[j] = [w * inv[j] for w in rows[j]]
    for j in reversed(block):
        for i in block:
            if i < j:
                rows[i] = [v - lower[j, i] * w for v, w in zip(rows[i], rows[j])]
    for j in block:
        for i in others:
            rows[i] = [v - far[i, j] * w for v, w in zip(rows[i], rows[j])]


def member_kernel(z_hbm, arr_ref, part_ref, rr_ref, w_ref, u_ref, p_ref,
                  w_out, coef_ref, back_ref,
                  base, tvec, code, zt, hi, lo, mat0, mat1, red0, red1, z_ref, hot_ref, sem):
    copy = pltpu.make_async_copy(z_hbm, z_ref, sem)
    copy.start()
    owners = arr_ref.shape[0]
    cap = arr_ref.shape[2] // 4
    fr = z_ref.shape[1]
    slots = z_ref.shape[0]
    p = p_ref[...]
    php = jnp.sum(part_ref[:, 0, :], axis=0, keepdims=True)[:, 0:1] + RIDGE * total(p * p)
    a = rr_ref[:, 0:1] / php
    w_out[...] = w_ref[...] + (u_ref[...] + a * p)
    for o in range(owners):
        got = arr_ref[o]
        base[:, o * cap:(o + 1) * cap] = got[:, 0:cap]
        tvec[:, o * cap:(o + 1) * cap] = got[:, cap:2 * cap]
        code[:, o * cap:(o + 1) * cap] = got[:, 2 * cap:3 * cap]
    prob = sigmoid(base[...] + a * tvec[...])
    curv = prob * (1.0 - prob)
    codes = code[...]
    label = jnp.where(codes >= 24.0, 1.0, 0.0)
    resid = prob - label
    local = codes - 16.0 - 8.0 * label
    at = lax.broadcasted_iota(jnp.int32, (MEM_DEV, slots), 0).astype(F32)
    onehot = jnp.where(local == at, 1.0, 0.0)

    copy.wait()
    z_t = z_ref[...].T
    zt[...] = z_t
    chunk = 512
    for c in range(0, slots, chunk):
        cz = zt[:, c:c + chunk].astype(F32) * curv[:, c:c + chunk]
        high = cz.astype(BF16)
        hi[:, c:c + chunk] = high
        lo[:, c:c + chunk] = (cz - high.astype(F32)).astype(BF16)
    mat, red = (mat0, mat1), (red0, red1)
    eye = jnp.where(lax.broadcasted_iota(jnp.int32, (fr, fr), 0)
                    == lax.broadcasted_iota(jnp.int32, (fr, fr), 1), RIDGE, 0.0)
    hot_ref[...] = onehot

    def one_gram(m, carry):
        mask = hot_ref[pl.ds(m, 1), :].astype(BF16)
        gram = dot_nn(hi[...] * mask, z_ref[...]) + dot_nn(lo[...] * mask, z_ref[...])
        put_lanes(mat, pl.ds(pl.multiple_of(m * fr, fr), fr), 0, gram + eye)
        return carry

    lax.fori_loop(0, MEM_DEV, one_gram, 0, unroll=GRAM_UNROLL)
    rm = resid * onehot
    rm_high = rm.astype(BF16)
    rm_low = (rm - rm_high.astype(F32)).astype(BF16)
    rhs = dot_nn(rm_high, z_ref[...]) + dot_nn(rm_low, z_ref[...])

    for k0 in range(0, fr, PANEL):
        lane0 = (k0 // 128) * 128
        orig = [get_lanes(mat, pl.ds(k0 + i, MEM_DEV, stride=fr), lane0) for i in range(PANEL)]
        wide = (MEM_DEV, 128)
        rows = [[o[:, c:c + 128] for c in range(0, o.shape[1], 128)]
                + [jnp.broadcast_to(rhs[:, k0 + i:k0 + i + 1], wide)]
                for i, o in enumerate(orig)]
        reduce_block(rows, k0 - lane0, range(BLOCK), range(BLOCK, PANEL))
        reduce_block(rows, k0 - lane0, range(BLOCK, PANEL), range(BLOCK))
        ys = [jnp.concatenate([r[-1]] * (len(r) - 1), axis=1) for r in rows]
        rows = [r[0] if len(r) == 2 else jnp.concatenate(r[:-1], axis=1) for r in rows]
        tail = rhs[:, lane0:]
        lanes = lax.broadcasted_iota(jnp.int32, tail.shape, 1) + lane0
        drop = jnp.zeros_like(tail)
        place = tail
        for i in range(PANEL):
            drop = drop + orig[i] * ys[i]
            place = jnp.where(lanes == k0 + i, ys[i], place)
        tail = jnp.where(lanes >= k0 + PANEL, tail - drop, place)
        rhs = tail if lane0 == 0 else jnp.concatenate([rhs[:, :lane0], tail], axis=1)
        for i in range(PANEL):
            put_lanes(red, slice((k0 + i) * MEM_DEV, (k0 + i + 1) * MEM_DEV), lane0, rows[i])
        top = k0 + PANEL
        if top < fr:
            lane1 = (top // 128) * 128
            row1 = lane1
            def trailing(m, carry, k0=k0, row1=row1, lane1=lane1):
                first = pl.multiple_of(m * fr, fr)
                o = get_lanes(mat, pl.ds(first + k0, PANEL), row1)
                w = get_lanes(red, pl.ds(k0 * MEM_DEV + m, PANEL, stride=MEM_DEV), lane1)
                o1, o2, o3 = three_parts(o)
                w1, w2, w3 = three_parts(w)
                left = jnp.concatenate([o1, o1, o2, o2, o1, o3], axis=0)
                right = jnp.concatenate([w1, w2, w1, w2, w3, w1], axis=0)
                rest = pl.ds(first + row1, fr - row1)
                put_lanes(mat, rest, lane1, get_lanes(mat, rest, lane1) - dot_tn(left, right))
                return carry

            lax.fori_loop(0, MEM_DEV, trailing, 0, unroll=UNROLL)

    lanes = lax.broadcasted_iota(jnp.int32, rhs.shape, 1)
    sol = jnp.where(lanes >= fr - PANEL, rhs, 0.0)
    for k0 in range(fr - 2 * PANEL, -1, -PANEL):
        new = sol
        lane0 = (k0 // 128) * 128
        for i in range(PANEL):
            w = get_lanes(red, slice((k0 + i) * MEM_DEV, (k0 + i + 1) * MEM_DEV), lane0)
            d = jnp.sum(w * sol[:, lane0:], axis=1, keepdims=True)
            new = jnp.where(lanes == k0 + i, rhs - d, new)
        sol = new
    coef = -sol
    coef_ref[...] = coef
    chigh = coef.astype(BF16)
    clow = (coef - chigh.astype(F32)).astype(BF16)
    scores = dot_nn(chigh, zt[...]) + dot_nn(clow, zt[...])
    back = jnp.sum(scores * onehot, axis=0, keepdims=True)
    for o in range(owners):
        back_ref[o] = back[:, o * cap:(o + 1) * cap]


def unpack_kernel(back_ref, slot_ref, out_ref):
    owners, _, cap = back_ref.shape
    back = back_ref[:, 0, :]
    hot_owner, hot_cap = owner_hot(slot_ref[...], owners, cap)
    rows = dot_tn(back, hot_owner, HIGH)
    out_ref[...] = jnp.sum(rows * hot_cap, axis=0, keepdims=True)


VMEM_LIMIT = 32 * 1024 * 1024
STAGE_LIMIT = 20 * 1024 * 1024


def on_chip(kernel, name, outs, *ins, scratch=()):
    vmem = pl.BlockSpec(memory_space=pltpu.VMEM)
    return pl.pallas_call(
        kernel,
        in_specs=[vmem] * len(ins),
        out_specs=[vmem] * len(outs),
        out_shape=[jax.ShapeDtypeStruct(s, d) for s, d in outs],
        scratch_shapes=list(scratch),
        compiler_params=pltpu.CompilerParams(vmem_limit_bytes=STAGE_LIMIT),
        name=name,
    )(*ins)


PH1 = ("core", "z")
PH2 = ("x", "y")


def on_device(features, re_features, member_id, slot, labels, offsets, feature_scale, w_start,
              *, sizes):
    n1 = sizes["core"] * sizes["z"]
    n2 = sizes["x"] * sizes["y"]
    n_mem = sizes["y"] * sizes["z"]
    n_grp = sizes["x"] * sizes["core"]
    rows, f = features.shape
    fr = re_features.shape[1]
    slots = 2 * rows
    cap = slots // n_mem
    def exchange(v, axes):
        return lax.all_to_all(v, axes, 0, 0, tiled=True)

    def reduce_rest(parts):
        got = exchange(parts, PH1)
        mid, = on_chip(again_kernel, "again", [((n2, 1, f), F32)], got)
        return exchange(mid, PH2)

    def reduce_permutes(v):
        half = sizes["z"] // 2
        def flip(index, size):
            return [(i, index(i)) for i in range(size)]
        nz = sizes["z"]
        phases = [
            ("x", sizes["x"], [lambda i, b=b: i ^ b for b in (1, 2, 3)]),
            ("y", sizes["y"], [lambda i, b=b: i ^ b for b in (1, 2, 3)]),
            (("core", "z"), n1, [lambda i, b=b: i ^ b for b in (nz, half, nz + half)]),
            ("z", nz, [lambda i, b=b: i ^ b for b in (1, 2, 3)]),
        ]
        for axes, size, maps in phases:
            moved = [lax.ppermute(v, axes, flip(index, size)) for index in maps]
            v, = on_chip(add_four_kernel, "add_four", [((1, 1, f), F32)], v, *moved)
        return v

    tmp = [pltpu.VMEM((8, f), BF16), pltpu.VMEM((8, rows), BF16)]
    vec = ((1, f), F32)
    small = ((1, 128), F32)
    row = ((1, rows), F32)
    parts = ((n1, 1, f), F32)
    vmem = pl.BlockSpec(memory_space=pltpu.VMEM)
    hbm = pl.BlockSpec(memory_space=pltpu.HBM)
    outs = [((1, rows), jnp.int32), row, row, row, vec, vec,
            ((1, 1, f), F32), row, row]
    packed, slot_row, code, lab, off, scale, w, gpart, score, curv = pl.pallas_call(
        start_kernel,
        in_specs=[hbm] * 8,
        out_specs=[hbm] + [vmem] * len(outs),
        out_shape=[pltpu.HBM((slots, fr), BF16)] + [jax.ShapeDtypeStruct(*o) for o in outs],
        scratch_shapes=[pltpu.VMEM((rows, f), BF16), pltpu.VMEM((rows, fr), BF16)] + [pltpu.VMEM((1, rows), jnp.int32)] * 2
        + [pltpu.VMEM((8, slots // 8, fr), BF16)] + tmp
        + [pltpu.SemaphoreType.DMA((7,)), pltpu.SemaphoreType.DMA((STEPS,)),
           pltpu.SemaphoreType.DMA((8,))],
        compiler_params=pltpu.CompilerParams(vmem_limit_bytes=STAGE_LIMIT),
        name="start",
    )(*[pltpu.with_memory_space_constraint(v, pltpu.HBM) for v in (
        features, re_features, slot.reshape(1, rows), member_id.reshape(1, rows),
        labels.reshape(1, rows), offsets.reshape(1, rows), feature_scale.reshape(1, f),
        w_start.reshape(1, f))])
    z_got = lax.all_to_all(packed.reshape(n_mem, cap, fr), ("y", "z"), 0, 0, tiled=True)
    z_got = z_got.reshape(slots, fr)
    for it in range(NEWTON):
        if it == 0:
            g2, z_got = lax.optimization_barrier((reduce_permutes(gpart), z_got))
        else:
            g2 = reduce_rest(gpart)
        if it == 0:
            x, hpart, p, rr, t = pl.pallas_call(
                cg_load_kernel,
                in_specs=[hbm] + [vmem] * 4,
                out_specs=[vmem] * 5,
                out_shape=[jax.ShapeDtypeStruct((rows, f), BF16)]
                + [jax.ShapeDtypeStruct(*o) for o in (parts, vec, small, row)],
                scratch_shapes=tmp + [pltpu.SemaphoreType.DMA((STEPS,))],
                compiler_params=pltpu.CompilerParams(vmem_limit_bytes=STAGE_LIMIT),
                name="cg_load",
            )(pltpu.with_memory_space_constraint(features, pltpu.HBM), g2, scale, w, curv)
        else:
            hpart, p, rr, t = on_chip(cg_first_kernel, "cg_first", [parts, vec, small, row],
                                      x, g2, scale, w, curv, scratch=tmp)
        h2 = reduce_rest(hpart)
        hpart, p, r, u, rr, t, m = on_chip(
            cg_next_kernel, "cg_next", [parts, vec, vec, vec, small, row, row],
            x, h2, scale, curv, p, rr, t, scratch=tmp)
        h2 = reduce_rest(hpart)
        ins = (x, h2, scale, curv, p, r, u, rr, t, m)
        if it + 1 < NEWTON:
            spart, p, u, rr, t, m = on_chip(
                cg_last_kernel, "cg_last", [((n1 * n2, 1, 128), F32), vec, vec, small, row, row],
                *ins, scratch=tmp)
            sgot = exchange(spart, ("x", "core", "y", "z"))
            gpart, w, score, curv = on_chip(
                grad_next_kernel, "grad_next", [parts, vec, row, row],
                x, sgot, rr, w, u, p, score, t, m, off, lab, scratch=tmp)
        else:
            send, p, u, rr = on_chip(
                cg_last_pack_kernel, "cg_last_pack",
                [((n_mem, 1, 4 * cap), F32), vec, vec, small],
                *ins, score, slot_row, code, scratch=[pltpu.VMEM((1, rows), F32)] + tmp)
    got = exchange(send, ("y", "z"))
    part, = on_chip(part_kernel, "part", [((n_grp, 1, 128), F32)], got)
    part = exchange(part, ("x", "core"))
    z_got = pltpu.with_memory_space_constraint(z_got, pltpu.HBM)
    w, member_coef, back = pl.pallas_call(
        member_kernel,
        in_specs=[pl.BlockSpec(memory_space=pltpu.HBM)] + [vmem] * 6,
        out_shape=[jax.ShapeDtypeStruct((1, f), F32),
                   jax.ShapeDtypeStruct((MEM_DEV, fr), F32),
                   jax.ShapeDtypeStruct((n_mem, 1, cap), F32)],
        scratch_shapes=[pltpu.VMEM((1, slots), F32)] * 3
        + [pltpu.VMEM((fr, slots), BF16)] * 3
        + [pltpu.VMEM((MEM_DEV * fr, 128), F32)] * 4
        + [pltpu.VMEM((slots, fr), BF16), pltpu.VMEM((MEM_DEV, slots), F32),
           pltpu.SemaphoreType.DMA(())],
        compiler_params=pltpu.CompilerParams(vmem_limit_bytes=VMEM_LIMIT),
        name="members",
    )(z_got, got, part, rr, w, u, p)
    returned = exchange(back, ("y", "z"))
    row_offsets = pl.pallas_call(
        unpack_kernel,
        out_shape=jax.ShapeDtypeStruct((1, rows), F32),
        compiler_params=pltpu.CompilerParams(vmem_limit_bytes=VMEM_LIMIT),
        name="unpack",
    )(returned, slot_row)
    return (w.reshape(f), member_coef, row_offsets.reshape(rows))


def solution(mesh):
    n_grp, n_mem = mesh.shape["grp"], mesh.shape["mem"]
    shape = {"x": n_grp // 2, "core": 2, "y": 4, "z": n_mem // 4}
    fine = Mesh(mesh.devices.reshape(tuple(shape.values())), tuple(shape))
    cut = P(("x", "core", "y", "z"))
    cut2 = P(("x", "core", "y", "z"), None)
    return jax.shard_map(
        functools.partial(on_device, sizes=shape),
        mesh=fine,
        in_specs=(cut2, cut2, cut, cut, cut, cut, P(), P()),
        out_specs=(P(), cut2, cut),
        check_vma=False,
    )
```

```python
import functools
import jax
import jax.numpy as jnp
from jax import lax
from jax.experimental import pallas as pl
from jax.experimental.pallas import tpu as pltpu
from jax.sharding import Mesh, PartitionSpec as P

MEM_DEV = 8
NEWTON = 2
RIDGE = 1.0
PANEL = 16
BLOCK = 8
STEPS = 4
F_STEPS = 4
B_STEPS = 2
UNROLL = 8
GRAMS = 2
F32 = jnp.float32
BF16 = jnp.bfloat16
HIGH = lax.Precision.HIGHEST


def dot_nn(a, b, precision=None):
    return lax.dot_general(a, b, (((1,), (0,)), ((), ())), precision=precision,
                           preferred_element_type=F32)


def dot_nt(a, b, precision=None):
    return lax.dot_general(a, b, (((1,), (1,)), ((), ())), precision=precision,
                           preferred_element_type=F32)


def dot_tn(a, b, precision=None):
    return lax.dot_general(a, b, (((0,), (0,)), ((), ())), precision=precision,
                           preferred_element_type=F32)


def split_rows(row):
    high = row.astype(BF16).astype(F32)
    low = row - high
    at = lax.broadcasted_iota(jnp.int32, (8, row.shape[1]), 0)
    return jnp.where(at == 0, high, jnp.where(at == 1, low, 0.0)).astype(BF16)


def sigmoid(x):
    return 1.0 / (1.0 + jnp.exp(-x))


def total(row):
    return jnp.sum(row, axis=1, keepdims=True)


def sum_parts(ref):
    acc = ref[0]
    for i in range(1, ref.shape[0]):
        acc = acc + ref[i]
    return acc


def forward(xs, x_ref, xs_ref, row_ref, arrive=None):
    xs_ref[...] = xs
    steps = F_STEPS if arrive is None else STEPS
    block = x_ref.shape[0] // steps

    def body(i, carry):
        at = pl.multiple_of(i * block, block)
        if arrive is not None:
            arrive(i, at, block)
        both = dot_nt(xs_ref[...], x_ref[pl.ds(at, block), :])
        row_ref[:, pl.ds(at, block)] = both[0:1] + both[1:2]
        return carry

    lax.fori_loop(0, steps, body, 0)
    return row_ref[...]


def backward(row, x_ref, split_ref, out_ref):
    split_ref[...] = split_rows(row)
    block = x_ref.shape[1] // B_STEPS

    def body(i, carry):
        at = pl.multiple_of(i * block, block)
        both = dot_nn(split_ref[...], x_ref[:, pl.ds(at, block)])
        val = both[0:1] + both[1:2]
        for j in range(out_ref.shape[0]):
            out_ref[j, :, pl.ds(at, block)] = val
        return carry

    lax.fori_loop(0, B_STEPS, body, 0)


def start_kernel(x_hbm, z_hbm, slot_hbm, member_hbm, lab_hbm, off_hbm, scale_hbm, w_hbm,
                 packed_ref, slot_ref, code_ref, lab_ref, off_ref, scale_ref, w_ref,
                 out_ref, score_ref, curv_ref,
                 x_ref, z_ref, member_ref, int_ref, buf, xs_ref, split_ref, sems, xsems, psems):
    pairs = [(slot_hbm, slot_ref), (z_hbm, z_ref), (scale_hbm, scale_ref), (w_hbm, w_ref),
             (member_hbm, member_ref), (lab_hbm, int_ref), (off_hbm, off_ref)]
    loads = [pltpu.make_async_copy(src, dst, sems.at[i]) for i, (src, dst) in enumerate(pairs)]
    for load in loads:
        load.start()

    def chunk(i, at, block):
        return pltpu.make_async_copy(x_hbm.at[pl.ds(at, block)], x_ref.at[pl.ds(at, block)],
                                     xsems.at[i])

    block = x_ref.shape[0] // STEPS
    for i in range(STEPS):
        chunk(i, i * block, block).start()
    loads[0].wait()
    loads[1].wait()
    size = buf.shape[1]

    def store(b):
        at = b * size if isinstance(b, int) else pl.multiple_of(b * size, size)
        return pltpu.make_async_copy(buf.at[b], packed_ref.at[pl.ds(at, size)], psems.at[b])

    def pack(b, carry):
        rows = lax.broadcasted_iota(jnp.int32, (size, slot_ref.shape[1]), 0) + b * size
        hot = jnp.where(rows == slot_ref[...], 1.0, 0.0).astype(BF16)
        buf[b] = dot_nn(hot, z_ref[...]).astype(BF16)
        store(b).start()
        return carry

    lax.fori_loop(0, buf.shape[0], pack, 0)
    for load in loads[2:]:
        load.wait()
    labels = int_ref[...]
    lab_ref[...] = labels.astype(F32)
    code_ref[...] = (member_ref[...] % MEM_DEV + 8 * labels + 16).astype(F32)
    score = forward(split_rows(scale_ref[...] * w_ref[...]), x_ref, xs_ref, score_ref,
                    lambda i, at, size: chunk(i, at, size).wait())
    prob = sigmoid(score + off_ref[...])
    curv_ref[...] = prob * (1.0 - prob)
    backward(prob - lab_ref[...], x_ref, split_ref, out_ref)
    for b in range(buf.shape[0]):
        store(b).wait()


def grad_next_kernel(x_ref, part_ref, rr_ref, w_ref, u_ref, p_ref, score_ref, t_ref, m_ref,
                     off_ref, lab_ref, out_ref, w_out, score_out, curv_ref, xs_ref, split_ref):
    a = last_coef(part_ref, rr_ref, p_ref)
    w_out[...] = w_ref[...] + (u_ref[...] + a * p_ref[...])
    score = score_ref[...] + (m_ref[...] + a * t_ref[...])
    prob = sigmoid(score + off_ref[...])
    score_out[...] = score
    curv_ref[...] = prob * (1.0 - prob)
    backward(prob - lab_ref[...], x_ref, split_ref, out_ref)


def last_coef(part_ref, rr_ref, p_ref):
    p = p_ref[...]
    php = jnp.sum(part_ref[:, 0, :], axis=0, keepdims=True)[:, 0:1] + RIDGE * total(p * p)
    return rr_ref[:, 0:1] / php


def cg_first_kernel(x_ref, sum_ref, scale_ref, w_ref, curv_ref, out_ref, p_out, rr_out, t_ref,
                    xs_ref, split_ref, arrive=None):
    r = -(scale_ref[...] * sum_parts(sum_ref) + RIDGE * w_ref[...])
    p_out[...] = r
    rr_out[...] = jnp.broadcast_to(total(r * r), rr_out.shape)
    t = forward(split_rows(scale_ref[...] * r), x_ref, xs_ref, t_ref, arrive)
    backward(curv_ref[...] * t, x_ref, split_ref, out_ref)


def cg_load_kernel(x_hbm, sum_ref, scale_ref, w_ref, curv_ref, x_ref, out_ref, p_out, rr_out,
                   t_ref, xs_ref, split_ref, sems):
    def chunk(i, at, block):
        return pltpu.make_async_copy(x_hbm.at[pl.ds(at, block)], x_ref.at[pl.ds(at, block)],
                                     sems.at[i])

    block = x_ref.shape[0] // STEPS
    for i in range(STEPS):
        chunk(i, i * block, block).start()
    cg_first_kernel(x_ref, sum_ref, scale_ref, w_ref, curv_ref, out_ref, p_out, rr_out, t_ref,
                    xs_ref, split_ref, lambda i, at, size: chunk(i, at, size).wait())


def cg_update(sum_ref, scale_ref, p_ref, r_ref, u_ref, rr_ref, p_out, r_out, u_out, rr_out):
    p = p_ref[...]
    q = scale_ref[...] * sum_parts(sum_ref) + RIDGE * p
    rr = rr_ref[:, 0:1]
    a = rr / total(p * q)
    u = a * p if u_ref is None else u_ref[...] + a * p
    r = r_ref[...] - a * q
    nn = total(r * r)
    p = r + (nn / rr) * p
    u_out[...] = u
    if r_out is not None:
        r_out[...] = r
    p_out[...] = p
    rr_out[...] = jnp.broadcast_to(nn, rr_out.shape)
    return a, split_rows(scale_ref[...] * p)


def cg_next_kernel(x_ref, sum_ref, scale_ref, curv_ref, p_ref, rr_ref, t_in,
                   out_ref, p_out, r_out, u_out, rr_out, t_ref, m_ref, xs_ref, split_ref):
    a, xs = cg_update(sum_ref, scale_ref, p_ref, p_ref, None, rr_ref, p_out, r_out, u_out, rr_out)
    m_ref[...] = a * t_in[...]
    t = forward(xs, x_ref, xs_ref, t_ref)
    backward(curv_ref[...] * t, x_ref, split_ref, out_ref)


def cg_last_kernel(x_ref, sum_ref, scale_ref, curv_ref, p_ref, r_ref, u_ref, rr_ref, t_in, m_in,
                   out_ref, p_out, u_out, rr_out, t_ref, m_ref, xs_ref, split_ref):
    a, xs = cg_update(sum_ref, scale_ref, p_ref, r_ref, u_ref, rr_ref, p_out, None, u_out, rr_out)
    m_ref[...] = m_in[...] + a * t_in[...]
    t = forward(xs, x_ref, xs_ref, t_ref)
    out_ref[...] = jnp.broadcast_to(total(curv_ref[...] * t * t).reshape(1, 1, 1), out_ref.shape)


def owner_hot(slot, owners, cap):
    rows = lax.broadcasted_iota(jnp.int32, (owners, slot.shape[1]), 0)
    hot_owner = jnp.where(rows == slot // cap, 1.0, 0.0)
    lanes = lax.broadcasted_iota(jnp.int32, (cap, slot.shape[1]), 0)
    hot_cap = jnp.where(lanes == slot % cap, 1.0, 0.0)
    return hot_owner, hot_cap


def cg_last_pack_kernel(x_ref, sum_ref, scale_ref, curv_ref, p_ref, r_ref, u_ref, rr_ref, t_in,
                        m_in, score_ref, slot_ref, code_ref, out_ref, p_out, u_out, rr_out,
                        t_ref, xs_ref, split_ref):
    a, xs = cg_update(sum_ref, scale_ref, p_ref, r_ref, u_ref, rr_ref, p_out, None, u_out, rr_out)
    owners, cap = out_ref.shape[0], out_ref.shape[2] // 4
    hot_owner, hot_cap = owner_hot(slot_ref[...], owners, cap)
    t = forward(xs, x_ref, xs_ref, t_ref)
    done = score_ref[...] + (m_in[...] + a * t_in[...])
    php = total(curv_ref[...] * t * t)
    left = jnp.concatenate([hot_owner * done, hot_owner * t, hot_owner * code_ref[...]], axis=0)
    send = dot_nt(left, hot_cap, HIGH)
    part = jnp.broadcast_to(php, (1, cap))
    for i in range(owners):
        out_ref[i] = jnp.concatenate(
            [send[j * owners + i:j * owners + i + 1] for j in range(3)] + [part], axis=1)


def again_kernel(sum_ref, out_ref):
    val = sum_parts(sum_ref)
    for i in range(out_ref.shape[0]):
        out_ref[i] = val


def add_kernel(*refs):
    out_ref = refs[-1]
    vals = [ref[...] for ref in refs[:-1]]
    while len(vals) > 1:
        vals = [vals[i] + vals[i + 1] for i in range(0, len(vals), 2)]
    out_ref[...] = vals[0]


def part_kernel(arr_ref, out_ref):
    last = arr_ref.shape[2] - 1
    got = arr_ref[:, 0, :]
    val = jnp.sum(got, axis=0, keepdims=True)[:, last:]
    out_ref[...] = jnp.broadcast_to(val.reshape(1, 1, 1), out_ref.shape)


def three_parts(v):
    a = v.astype(BF16)
    rest = v - a.astype(F32)
    b = rest.astype(BF16)
    c = (rest - b.astype(F32)).astype(BF16)
    return a, b, c


def get_lanes(halves, rows, lane):
    if lane:
        return halves[1][rows, :]
    return jnp.concatenate([halves[0][rows, :], halves[1][rows, :]], axis=1)


def put_lanes(halves, rows, lane, value):
    if lane:
        halves[1][rows, :] = value
    else:
        halves[0][rows, :] = value[:, :128]
        halves[1][rows, :] = value[:, 128:]


def reduce_block(rows, lane, block, others):
    def at(i, j):
        return jnp.broadcast_to(rows[i][0][:, lane + j:lane + j + 1], rows[i][0].shape)

    block, others = list(block), list(others)
    c = {(i, j): at(i, j) for i in block for j in block if j <= i}
    far = {(i, j): at(i, j) for i in others for j in block}
    lower, inv = {}, {}
    for j in block:
        inv[j] = 1.0 / c[j, j]
        for i in block:
            if i > j:
                lower[i, j] = c[i, j] * inv[j]
        for i in block:
            for k in block:
                if j < k <= i:
                    c[i, k] = c[i, k] - lower[i, j] * c[k, j]
    for j in block:
        for i in block:
            if i > j:
                rows[i] = [v - lower[i, j] * w for v, w in zip(rows[i], rows[j])]
    for j in block:
        rows[j] = [w * inv[j] for w in rows[j]]
    for j in reversed(block):
        for i in block:
            if i < j:
                rows[i] = [v - lower[j, i] * w for v, w in zip(rows[i], rows[j])]
    for j in block:
        for i in others:
            rows[i] = [v - far[i, j] * w for v, w in zip(rows[i], rows[j])]


def member_kernel(z_hbm, arr_ref, part_ref, rr_ref, w_ref, u_ref, p_ref,
                  w_out, coef_ref, back_ref,
                  base, tvec, code, zt, hi, lo, mat0, mat1, red0, red1, z_ref, hot_ref,
                  left_ref, sem):
    copy = pltpu.make_async_copy(z_hbm, z_ref, sem)
    copy.start()
    owners = arr_ref.shape[0]
    cap = arr_ref.shape[2] // 4
    fr = z_ref.shape[1]
    slots = z_ref.shape[0]
    p = p_ref[...]
    php = jnp.sum(part_ref[:, 0, :], axis=0, keepdims=True)[:, 0:1] + RIDGE * total(p * p)
    a = rr_ref[:, 0:1] / php
    w_out[...] = w_ref[...] + (u_ref[...] + a * p)
    for o in range(owners):
        got = arr_ref[o]
        base[:, o * cap:(o + 1) * cap] = got[:, 0:cap]
        tvec[:, o * cap:(o + 1) * cap] = got[:, cap:2 * cap]
        code[:, o * cap:(o + 1) * cap] = got[:, 2 * cap:3 * cap]
    prob = sigmoid(base[...] + a * tvec[...])
    curv = prob * (1.0 - prob)
    codes = code[...]
    label = jnp.where(codes >= 24.0, 1.0, 0.0)
    resid = prob - label
    local = codes - 16.0 - 8.0 * label
    at = lax.broadcasted_iota(jnp.int32, (MEM_DEV, slots), 0).astype(F32)
    onehot = jnp.where(local == at, 1.0, 0.0)

    copy.wait()
    z_t = z_ref[...].T
    zt[...] = z_t
    chunk = 512
    for c in range(0, slots, chunk):
        cz = zt[:, c:c + chunk].astype(F32) * curv[:, c:c + chunk]
        high = cz.astype(BF16)
        hi[:, c:c + chunk] = high
        lo[:, c:c + chunk] = (cz - high.astype(F32)).astype(BF16)
    mat, red = (mat0, mat1), (red0, red1)
    eye = jnp.where(lax.broadcasted_iota(jnp.int32, (fr, fr), 0)
                    == lax.broadcasted_iota(jnp.int32, (fr, fr), 1), RIDGE, 0.0)
    hot_ref[...] = onehot

    def some_grams(step, carry):
        for j in range(GRAMS):
            mask = hot_ref[pl.ds(step * GRAMS + j, 1), :].astype(BF16)
            left_ref[2 * j * fr:(2 * j + 1) * fr, :] = hi[...] * mask
            left_ref[(2 * j + 1) * fr:(2 * j + 2) * fr, :] = lo[...] * mask
        both = dot_nn(left_ref[...], z_ref[...])
        for j in range(GRAMS):
            gram = both[2 * j * fr:(2 * j + 1) * fr] + both[(2 * j + 1) * fr:(2 * j + 2) * fr]
            at = pl.multiple_of((step * GRAMS + j) * fr, fr)
            put_lanes(mat, pl.ds(at, fr), 0, gram + eye)
        return carry

    lax.fori_loop(0, MEM_DEV // GRAMS, some_grams, 0)
    rm = resid * onehot
    rm_high = rm.astype(BF16)
    rm_low = (rm - rm_high.astype(F32)).astype(BF16)
    rhs = dot_nn(rm_high, z_ref[...]) + dot_nn(rm_low, z_ref[...])

    for k0 in range(0, fr, PANEL):
        lane0 = (k0 // 128) * 128
        orig = [get_lanes(mat, pl.ds(k0 + i, MEM_DEV, stride=fr), lane0) for i in range(PANEL)]
        wide = (MEM_DEV, 128)
        rows = [[o[:, c:c + 128] for c in range(0, o.shape[1], 128)]
                + [jnp.broadcast_to(rhs[:, k0 + i:k0 + i + 1], wide)]
                for i, o in enumerate(orig)]
        reduce_block(rows, k0 - lane0, range(BLOCK), range(BLOCK, PANEL))
        reduce_block(rows, k0 - lane0, range(BLOCK, PANEL), range(BLOCK))
        ys = [jnp.concatenate([r[-1]] * (len(r) - 1), axis=1) for r in rows]
        rows = [r[0] if len(r) == 2 else jnp.concatenate(r[:-1], axis=1) for r in rows]
        tail = rhs[:, lane0:]
        lanes = lax.broadcasted_iota(jnp.int32, tail.shape, 1) + lane0
        drop = jnp.zeros_like(tail)
        place = tail
        for i in range(PANEL):
            drop = drop + orig[i] * ys[i]
            place = jnp.where(lanes == k0 + i, ys[i], place)
        tail = jnp.where(lanes >= k0 + PANEL, tail - drop, place)
        rhs = tail if lane0 == 0 else jnp.concatenate([rhs[:, :lane0], tail], axis=1)
        for i in range(PANEL):
            put_lanes(red, slice((k0 + i) * MEM_DEV, (k0 + i + 1) * MEM_DEV), lane0, rows[i])
        top = k0 + PANEL
        if top < fr:
            lane1 = (top // 128) * 128
            row1 = lane1
            def trailing(m, carry, k0=k0, row1=row1, lane1=lane1):
                first = pl.multiple_of(m * fr, fr)
                o = get_lanes(mat, pl.ds(first + k0, PANEL), row1)
                w = get_lanes(red, pl.ds(k0 * MEM_DEV + m, PANEL, stride=MEM_DEV), lane1)
                o1, o2, o3 = three_parts(o)
                w1, w2, w3 = three_parts(w)
                left = jnp.concatenate([o1, o1, o2, o2, o1, o3], axis=0)
                right = jnp.concatenate([w1, w2, w1, w2, w3, w1], axis=0)
                rest = pl.ds(first + row1, fr - row1)
                put_lanes(mat, rest, lane1, get_lanes(mat, rest, lane1) - dot_tn(left, right))
                return carry

            lax.fori_loop(0, MEM_DEV, trailing, 0, unroll=UNROLL)

    lanes = lax.broadcasted_iota(jnp.int32, rhs.shape, 1)
    sol = jnp.where(lanes >= fr - PANEL, rhs, 0.0)
    for k0 in range(fr - 2 * PANEL, -1, -PANEL):
        new = sol
        lane0 = (k0 // 128) * 128
        for i in range(PANEL):
            w = get_lanes(red, slice((k0 + i) * MEM_DEV, (k0 + i + 1) * MEM_DEV), lane0)
            d = jnp.sum(w * sol[:, lane0:], axis=1, keepdims=True)
            new = jnp.where(lanes == k0 + i, rhs - d, new)
        sol = new
    coef = -sol
    coef_ref[...] = coef
    chigh = coef.astype(BF16)
    clow = (coef - chigh.astype(F32)).astype(BF16)
    scores = dot_nn(chigh, zt[...]) + dot_nn(clow, zt[...])
    back = jnp.sum(scores * onehot, axis=0, keepdims=True)
    for o in range(owners):
        back_ref[o] = back[:, o * cap:(o + 1) * cap]


def unpack_kernel(back_ref, slot_ref, out_ref):
    owners, _, cap = back_ref.shape
    back = back_ref[:, 0, :]
    hot_owner, hot_cap = owner_hot(slot_ref[...], owners, cap)
    rows = dot_tn(back, hot_owner, HIGH)
    out_ref[...] = jnp.sum(rows * hot_cap, axis=0, keepdims=True)


VMEM_LIMIT = 32 * 1024 * 1024
STAGE_LIMIT = 20 * 1024 * 1024


def on_chip(kernel, name, outs, *ins, scratch=()):
    vmem = pl.BlockSpec(memory_space=pltpu.VMEM)
    return pl.pallas_call(
        kernel,
        in_specs=[vmem] * len(ins),
        out_specs=[vmem] * len(outs),
        out_shape=[jax.ShapeDtypeStruct(s, d) for s, d in outs],
        scratch_shapes=list(scratch),
        compiler_params=pltpu.CompilerParams(vmem_limit_bytes=STAGE_LIMIT),
        name=name,
    )(*ins)


PH1 = ("core", "z")
PH2 = ("x", "y")


def on_device(features, re_features, member_id, slot, labels, offsets, feature_scale, w_start,
              *, sizes):
    n1 = sizes["core"] * sizes["z"]
    n2 = sizes["x"] * sizes["y"]
    n_mem = sizes["y"] * sizes["z"]
    n_grp = sizes["x"] * sizes["core"]
    rows, f = features.shape
    fr = re_features.shape[1]
    slots = 2 * rows
    cap = slots // n_mem
    def exchange(v, axes):
        return lax.all_to_all(v, axes, 0, 0, tiled=True)

    def reduce_rest(parts):
        got = exchange(parts, PH1)
        mid, = on_chip(again_kernel, "again", [((n2, 1, f), F32)], got)
        return exchange(mid, PH2)

    def reduce_permutes(v):
        half = sizes["z"] // 2
        four = (1, 2, 3)
        for axis, flips in (("x", four), ("core", (1,)), ("y", four), ("z", four), ("z", (half,))):
            size = sizes[axis]
            moved = [lax.ppermute(v, axis, [(i, i ^ b) for i in range(size)]) for b in flips]
            v, = on_chip(add_kernel, "add", [((1, 1, f), F32)], v, *moved)
        return v

    tmp = [pltpu.VMEM((8, f), BF16), pltpu.VMEM((8, rows), BF16)]
    vec = ((1, f), F32)
    small = ((1, 128), F32)
    row = ((1, rows), F32)
    parts = ((n1, 1, f), F32)
    vmem = pl.BlockSpec(memory_space=pltpu.VMEM)
    hbm = pl.BlockSpec(memory_space=pltpu.HBM)
    outs = [((1, rows), jnp.int32), row, row, row, vec, vec,
            ((1, 1, f), F32), row, row]
    packed, slot_row, code, lab, off, scale, w, gpart, score, curv = pl.pallas_call(
        start_kernel,
        in_specs=[hbm] * 8,
        out_specs=[hbm] + [vmem] * len(outs),
        out_shape=[pltpu.HBM((slots, fr), BF16)] + [jax.ShapeDtypeStruct(*o) for o in outs],
        scratch_shapes=[pltpu.VMEM((rows, f), BF16), pltpu.VMEM((rows, fr), BF16)] + [pltpu.VMEM((1, rows), jnp.int32)] * 2
        + [pltpu.VMEM((8, slots // 8, fr), BF16)] + tmp
        + [pltpu.SemaphoreType.DMA((7,)), pltpu.SemaphoreType.DMA((STEPS,)),
           pltpu.SemaphoreType.DMA((8,))],
        compiler_params=pltpu.CompilerParams(vmem_limit_bytes=STAGE_LIMIT),
        name="start",
    )(*[pltpu.with_memory_space_constraint(v, pltpu.HBM) for v in (
        features, re_features, slot.reshape(1, rows), member_id.reshape(1, rows),
        labels.reshape(1, rows), offsets.reshape(1, rows), feature_scale.reshape(1, f),
        w_start.reshape(1, f))])
    z_got = lax.all_to_all(packed.reshape(n_mem, cap, fr), ("y", "z"), 0, 0, tiled=True)
    z_got = z_got.reshape(slots, fr)
    for it in range(NEWTON):
        if it == 0:
            g2, z_got = lax.optimization_barrier((reduce_permutes(gpart), z_got))
        else:
            g2 = reduce_rest(gpart)
        if it == 0:
            x, hpart, p, rr, t = pl.pallas_call(
                cg_load_kernel,
                in_specs=[hbm] + [vmem] * 4,
                out_specs=[vmem] * 5,
                out_shape=[jax.ShapeDtypeStruct((rows, f), BF16)]
                + [jax.ShapeDtypeStruct(*o) for o in (parts, vec, small, row)],
                scratch_shapes=tmp + [pltpu.SemaphoreType.DMA((STEPS,))],
                compiler_params=pltpu.CompilerParams(vmem_limit_bytes=STAGE_LIMIT),
                name="cg_load",
            )(pltpu.with_memory_space_constraint(features, pltpu.HBM), g2, scale, w, curv)
        else:
            hpart, p, rr, t = on_chip(cg_first_kernel, "cg_first", [parts, vec, small, row],
                                      x, g2, scale, w, curv, scratch=tmp)
        h2 = reduce_rest(hpart)
        hpart, p, r, u, rr, t, m = on_chip(
            cg_next_kernel, "cg_next", [parts, vec, vec, vec, small, row, row],
            x, h2, scale, curv, p, rr, t, scratch=tmp)
        h2 = reduce_rest(hpart)
        ins = (x, h2, scale, curv, p, r, u, rr, t, m)
        if it + 1 < NEWTON:
            spart, p, u, rr, t, m = on_chip(
                cg_last_kernel, "cg_last", [((n1 * n2, 1, 128), F32), vec, vec, small, row, row],
                *ins, scratch=tmp)
            sgot = exchange(spart, ("x", "core", "y", "z"))
            gpart, w, score, curv = on_chip(
                grad_next_kernel, "grad_next", [parts, vec, row, row],
                x, sgot, rr, w, u, p, score, t, m, off, lab, scratch=tmp)
        else:
            send, p, u, rr = on_chip(
                cg_last_pack_kernel, "cg_last_pack",
                [((n_mem, 1, 4 * cap), F32), vec, vec, small],
                *ins, score, slot_row, code, scratch=[pltpu.VMEM((1, rows), F32)] + tmp)
    got = exchange(send, ("y", "z"))
    part, = on_chip(part_kernel, "part", [((n_grp, 1, 128), F32)], got)
    part = exchange(part, ("x", "core"))
    z_got = pltpu.with_memory_space_constraint(z_got, pltpu.HBM)
    w, member_coef, back = pl.pallas_call(
        member_kernel,
        in_specs=[pl.BlockSpec(memory_space=pltpu.HBM)] + [vmem] * 6,
        out_shape=[jax.ShapeDtypeStruct((1, f), F32),
                   jax.ShapeDtypeStruct((MEM_DEV, fr), F32),
                   jax.ShapeDtypeStruct((n_mem, 1, cap), F32)],
        scratch_shapes=[pltpu.VMEM((1, slots), F32)] * 3
        + [pltpu.VMEM((fr, slots), BF16)] * 3
        + [pltpu.VMEM((MEM_DEV * fr, 128), F32)] * 4
        + [pltpu.VMEM((slots, fr), BF16), pltpu.VMEM((MEM_DEV, slots), F32),
           pltpu.VMEM((2 * GRAMS * fr, slots), BF16),
           pltpu.SemaphoreType.DMA(())],
        compiler_params=pltpu.CompilerParams(vmem_limit_bytes=VMEM_LIMIT),
        name="members",
    )(z_got, got, part, rr, w, u, p)
    returned = exchange(back, ("y", "z"))
    row_offsets = pl.pallas_call(
        unpack_kernel,
        out_shape=jax.ShapeDtypeStruct((1, rows), F32),
        compiler_params=pltpu.CompilerParams(vmem_limit_bytes=VMEM_LIMIT),
        name="unpack",
    )(returned, slot_row)
    return (w.reshape(f), member_coef, row_offsets.reshape(rows))


def solution(mesh):
    n_grp, n_mem = mesh.shape["grp"], mesh.shape["mem"]
    shape = {"x": n_grp // 2, "core": 2, "y": 4, "z": n_mem // 4}
    fine = Mesh(mesh.devices.reshape(tuple(shape.values())), tuple(shape))
    cut = P(("x", "core", "y", "z"))
    cut2 = P(("x", "core", "y", "z"), None)
    return jax.shard_map(
        functools.partial(on_device, sizes=shape),
        mesh=fine,
        in_specs=(cut2, cut2, cut, cut, cut, cut, P(), P()),
        out_specs=(P(), cut2, cut),
        check_vma=False,
    )
```

```python
import functools
import jax
import jax.numpy as jnp
from jax import lax
from jax.experimental import pallas as pl
from jax.experimental.pallas import tpu as pltpu
from jax.sharding import Mesh, PartitionSpec as P

MEM_DEV = 8
NEWTON = 2
RIDGE = 1.0
PANEL = 16
BLOCK = 8
STEPS = 4
F_STEPS = 2
B_STEPS = 2
GRAMS = 2
F32 = jnp.float32
BF16 = jnp.bfloat16
HIGH = lax.Precision.HIGHEST


def dot_nn(a, b, precision=None):
    return lax.dot_general(a, b, (((1,), (0,)), ((), ())), precision=precision,
                           preferred_element_type=F32)


def dot_nt(a, b, precision=None):
    return lax.dot_general(a, b, (((1,), (1,)), ((), ())), precision=precision,
                           preferred_element_type=F32)


def dot_tn(a, b, precision=None):
    return lax.dot_general(a, b, (((0,), (0,)), ((), ())), precision=precision,
                           preferred_element_type=F32)


def split_rows(row):
    high = row.astype(BF16).astype(F32)
    low = row - high
    at = lax.broadcasted_iota(jnp.int32, (8, row.shape[1]), 0)
    return jnp.where(at == 0, high, jnp.where(at == 1, low, 0.0)).astype(BF16)


def sigmoid(x):
    return 1.0 / (1.0 + jnp.exp(-x))


def total(row):
    return jnp.sum(row, axis=1, keepdims=True)


def sum_parts(ref):
    acc = ref[0]
    for i in range(1, ref.shape[0]):
        acc = acc + ref[i]
    return acc


def forward(xs, x_ref, xs_ref, row_ref, arrive=None, steps=STEPS):
    xs_ref[...] = xs
    block = x_ref.shape[0] // steps

    def body(i, carry):
        at = pl.multiple_of(i * block, block)
        if arrive is not None:
            arrive(i, at, block)
        both = dot_nt(xs_ref[...], x_ref[pl.ds(at, block), :])
        row_ref[:, pl.ds(at, block)] = both[0:1] + both[1:2]
        return carry

    lax.fori_loop(0, steps, body, 0)
    return row_ref[...]


def backward(row, x_ref, split_ref, out_ref):
    split_ref[...] = split_rows(row)
    block = x_ref.shape[1] // B_STEPS

    def body(i, carry):
        at = pl.multiple_of(i * block, block)
        both = dot_nn(split_ref[...], x_ref[:, pl.ds(at, block)])
        val = both[0:1] + both[1:2]
        for j in range(out_ref.shape[0]):
            out_ref[j, :, pl.ds(at, block)] = val
        return carry

    lax.fori_loop(0, B_STEPS, body, 0)


def start_kernel(x_hbm, z_hbm, slot_hbm, member_hbm, lab_hbm, off_hbm, scale_hbm, w_hbm,
                 packed_ref, slot_ref, code_ref, lab_ref, off_ref, scale_ref, w_ref,
                 out_ref, score_ref, curv_ref,
                 x_ref, z_ref, member_ref, int_ref, buf, xs_ref, split_ref, sems, xsems, psems):
    pairs = [(slot_hbm, slot_ref), (z_hbm, z_ref), (scale_hbm, scale_ref), (w_hbm, w_ref),
             (member_hbm, member_ref), (lab_hbm, int_ref), (off_hbm, off_ref)]
    loads = [pltpu.make_async_copy(src, dst, sems.at[i]) for i, (src, dst) in enumerate(pairs)]
    for load in loads:
        load.start()

    def chunk(i, at, block):
        return pltpu.make_async_copy(x_hbm.at[pl.ds(at, block)], x_ref.at[pl.ds(at, block)],
                                     xsems.at[i])

    block = x_ref.shape[0] // STEPS
    for i in range(STEPS):
        chunk(i, i * block, block).start()
    loads[0].wait()
    loads[1].wait()
    size = buf.shape[1]

    def store(b):
        at = b * size if isinstance(b, int) else pl.multiple_of(b * size, size)
        return pltpu.make_async_copy(buf.at[b], packed_ref.at[pl.ds(at, size)], psems.at[b])

    def pack(b, carry):
        rows = lax.broadcasted_iota(jnp.int32, (size, slot_ref.shape[1]), 0) + b * size
        hot = jnp.where(rows == slot_ref[...], 1.0, 0.0).astype(BF16)
        buf[b] = dot_nn(hot, z_ref[...]).astype(BF16)
        store(b).start()
        return carry

    lax.fori_loop(0, buf.shape[0], pack, 0)
    for load in loads[2:]:
        load.wait()
    labels = int_ref[...]
    lab_ref[...] = labels.astype(F32)
    code_ref[...] = (member_ref[...] % MEM_DEV + 8 * labels + 16).astype(F32)
    score = forward(split_rows(scale_ref[...] * w_ref[...]), x_ref, xs_ref, score_ref,
                    lambda i, at, size: chunk(i, at, size).wait())
    prob = sigmoid(score + off_ref[...])
    curv_ref[...] = prob * (1.0 - prob)
    backward(prob - lab_ref[...], x_ref, split_ref, out_ref)
    for b in range(buf.shape[0]):
        store(b).wait()


def grad_next_kernel(x_ref, part_ref, rr_ref, w_ref, u_ref, p_ref, score_ref, t_ref, m_ref,
                     off_ref, lab_ref, out_ref, w_out, score_out, curv_ref, xs_ref, split_ref):
    a = last_coef(part_ref, rr_ref, p_ref)
    w_out[...] = w_ref[...] + (u_ref[...] + a * p_ref[...])
    score = score_ref[...] + (m_ref[...] + a * t_ref[...])
    prob = sigmoid(score + off_ref[...])
    score_out[...] = score
    curv_ref[...] = prob * (1.0 - prob)
    backward(prob - lab_ref[...], x_ref, split_ref, out_ref)


def last_coef(part_ref, rr_ref, p_ref):
    p = p_ref[...]
    php = jnp.sum(part_ref[:, 0, :], axis=0, keepdims=True)[:, 0:1] + RIDGE * total(p * p)
    return rr_ref[:, 0:1] / php


def cg_first_kernel(x_ref, sum_ref, scale_ref, w_ref, curv_ref, out_ref, p_out, rr_out, t_ref,
                    xs_ref, split_ref, arrive=None):
    r = -(scale_ref[...] * sum_parts(sum_ref) + RIDGE * w_ref[...])
    p_out[...] = r
    rr_out[...] = jnp.broadcast_to(total(r * r), rr_out.shape)
    t = forward(split_rows(scale_ref[...] * r), x_ref, xs_ref, t_ref, arrive,
                STEPS if arrive else F_STEPS)
    backward(curv_ref[...] * t, x_ref, split_ref, out_ref)


def cg_load_kernel(x_hbm, sum_ref, scale_ref, w_ref, curv_ref, x_ref, out_ref, p_out, rr_out,
                   t_ref, xs_ref, split_ref, sems):
    def chunk(i, at, block):
        return pltpu.make_async_copy(x_hbm.at[pl.ds(at, block)], x_ref.at[pl.ds(at, block)],
                                     sems.at[i])

    block = x_ref.shape[0] // STEPS
    for i in range(STEPS):
        chunk(i, i * block, block).start()
    cg_first_kernel(x_ref, sum_ref, scale_ref, w_ref, curv_ref, out_ref, p_out, rr_out, t_ref,
                    xs_ref, split_ref, lambda i, at, size: chunk(i, at, size).wait())


def cg_update(sum_ref, scale_ref, p_ref, r_ref, u_ref, rr_ref, p_out, r_out, u_out, rr_out):
    p = p_ref[...]
    q = scale_ref[...] * sum_parts(sum_ref) + RIDGE * p
    rr = rr_ref[:, 0:1]
    a = rr / total(p * q)
    u = a * p if u_ref is None else u_ref[...] + a * p
    r = r_ref[...] - a * q
    nn = total(r * r)
    p = r + (nn / rr) * p
    u_out[...] = u
    if r_out is not None:
        r_out[...] = r
    p_out[...] = p
    rr_out[...] = jnp.broadcast_to(nn, rr_out.shape)
    return a, split_rows(scale_ref[...] * p)


def cg_next_kernel(x_ref, sum_ref, scale_ref, curv_ref, p_ref, rr_ref, t_in,
                   out_ref, p_out, r_out, u_out, rr_out, t_ref, m_ref, xs_ref, split_ref):
    a, xs = cg_update(sum_ref, scale_ref, p_ref, p_ref, None, rr_ref, p_out, r_out, u_out, rr_out)
    m_ref[...] = a * t_in[...]
    t = forward(xs, x_ref, xs_ref, t_ref, steps=F_STEPS)
    backward(curv_ref[...] * t, x_ref, split_ref, out_ref)


def cg_last_kernel(x_ref, sum_ref, scale_ref, curv_ref, p_ref, r_ref, u_ref, rr_ref, t_in, m_in,
                   out_ref, p_out, u_out, rr_out, t_ref, m_ref, xs_ref, split_ref):
    a, xs = cg_update(sum_ref, scale_ref, p_ref, r_ref, u_ref, rr_ref, p_out, None, u_out, rr_out)
    m_ref[...] = m_in[...] + a * t_in[...]
    t = forward(xs, x_ref, xs_ref, t_ref)
    out_ref[...] = jnp.broadcast_to(total(curv_ref[...] * t * t).reshape(1, 1, 1), out_ref.shape)


def owner_hot(slot, owners, cap):
    rows = lax.broadcasted_iota(jnp.int32, (owners, slot.shape[1]), 0)
    hot_owner = jnp.where(rows == slot // cap, 1.0, 0.0)
    lanes = lax.broadcasted_iota(jnp.int32, (cap, slot.shape[1]), 0)
    hot_cap = jnp.where(lanes == slot % cap, 1.0, 0.0)
    return hot_owner, hot_cap


def cg_last_pack_kernel(x_ref, sum_ref, scale_ref, curv_ref, p_ref, r_ref, u_ref, rr_ref, t_in,
                        m_in, score_ref, slot_ref, code_ref, out_ref, p_out, u_out, rr_out,
                        t_ref, xs_ref, split_ref):
    a, xs = cg_update(sum_ref, scale_ref, p_ref, r_ref, u_ref, rr_ref, p_out, None, u_out, rr_out)
    owners, cap = out_ref.shape[0], out_ref.shape[2] // 4
    hot_owner, hot_cap = owner_hot(slot_ref[...], owners, cap)
    t = forward(xs, x_ref, xs_ref, t_ref)
    done = score_ref[...] + (m_in[...] + a * t_in[...])
    php = total(curv_ref[...] * t * t)
    left = jnp.concatenate([hot_owner * done, hot_owner * t, hot_owner * code_ref[...]], axis=0)
    send = dot_nt(left, hot_cap, HIGH)
    part = jnp.broadcast_to(php, (1, cap))
    for i in range(owners):
        out_ref[i] = jnp.concatenate(
            [send[j * owners + i:j * owners + i + 1] for j in range(3)] + [part], axis=1)


def again_kernel(sum_ref, out_ref):
    val = sum_parts(sum_ref)
    for i in range(out_ref.shape[0]):
        out_ref[i] = val


def add_kernel(*refs):
    out_ref = refs[-1]
    vals = [ref[...] for ref in refs[:-1]]
    while len(vals) > 1:
        vals = [vals[i] + vals[i + 1] for i in range(0, len(vals), 2)]
    out_ref[...] = vals[0]


def part_kernel(arr_ref, out_ref):
    last = arr_ref.shape[2] - 1
    got = arr_ref[:, 0, :]
    val = jnp.sum(got, axis=0, keepdims=True)[:, last:]
    out_ref[...] = jnp.broadcast_to(val.reshape(1, 1, 1), out_ref.shape)


def three_parts(v):
    a = v.astype(BF16)
    rest = v - a.astype(F32)
    b = rest.astype(BF16)
    c = (rest - b.astype(F32)).astype(BF16)
    return a, b, c


def get_lanes(halves, rows, lane):
    if lane:
        return halves[1][rows, :]
    return jnp.concatenate([halves[0][rows, :], halves[1][rows, :]], axis=1)


def put_lanes(halves, rows, lane, value):
    if lane:
        halves[1][rows, :] = value
    else:
        halves[0][rows, :] = value[:, :128]
        halves[1][rows, :] = value[:, 128:]


def reduce_block(rows, lane, block, others):
    def at(i, j):
        return jnp.broadcast_to(rows[i][0][:, lane + j:lane + j + 1], rows[i][0].shape)

    block, others = list(block), list(others)
    c = {(i, j): at(i, j) for i in block for j in block if j <= i}
    far = {(i, j): at(i, j) for i in others for j in block}
    lower, inv = {}, {}
    for j in block:
        inv[j] = 1.0 / c[j, j]
        for i in block:
            if i > j:
                lower[i, j] = c[i, j] * inv[j]
        for i in block:
            for k in block:
                if j < k <= i:
                    c[i, k] = c[i, k] - lower[i, j] * c[k, j]
    for j in block:
        for i in block:
            if i > j:
                rows[i] = [v - lower[i, j] * w for v, w in zip(rows[i], rows[j])]
    for j in block:
        rows[j] = [w * inv[j] for w in rows[j]]
    for j in reversed(block):
        for i in block:
            if i < j:
                rows[i] = [v - lower[j, i] * w for v, w in zip(rows[i], rows[j])]
    for j in block:
        for i in others:
            rows[i] = [v - far[i, j] * w for v, w in zip(rows[i], rows[j])]


def member_kernel(z_hbm, arr_ref, part_ref, rr_ref, w_ref, u_ref, p_ref,
                  w_out, coef_ref, back_ref,
                  base, tvec, code, zt, hi, lo, mat0, mat1, red0, red1, z_ref, hot_ref,
                  left_ref, sem):
    copy = pltpu.make_async_copy(z_hbm, z_ref, sem)
    copy.start()
    owners = arr_ref.shape[0]
    cap = arr_ref.shape[2] // 4
    fr = z_ref.shape[1]
    slots = z_ref.shape[0]
    p = p_ref[...]
    php = jnp.sum(part_ref[:, 0, :], axis=0, keepdims=True)[:, 0:1] + RIDGE * total(p * p)
    a = rr_ref[:, 0:1] / php
    w_out[...] = w_ref[...] + (u_ref[...] + a * p)
    for o in range(owners):
        got = arr_ref[o]
        base[:, o * cap:(o + 1) * cap] = got[:, 0:cap]
        tvec[:, o * cap:(o + 1) * cap] = got[:, cap:2 * cap]
        code[:, o * cap:(o + 1) * cap] = got[:, 2 * cap:3 * cap]
    prob = sigmoid(base[...] + a * tvec[...])
    curv = prob * (1.0 - prob)
    codes = code[...]
    label = jnp.where(codes >= 24.0, 1.0, 0.0)
    resid = prob - label
    local = codes - 16.0 - 8.0 * label
    at = lax.broadcasted_iota(jnp.int32, (MEM_DEV, slots), 0).astype(F32)
    onehot = jnp.where(local == at, 1.0, 0.0)

    copy.wait()
    z_t = z_ref[...].T
    zt[...] = z_t
    chunk = 512
    for c in range(0, slots, chunk):
        cz = zt[:, c:c + chunk].astype(F32) * curv[:, c:c + chunk]
        high = cz.astype(BF16)
        hi[:, c:c + chunk] = high
        lo[:, c:c + chunk] = (cz - high.astype(F32)).astype(BF16)
    mat, red = (mat0, mat1), (red0, red1)
    eye = jnp.where(lax.broadcasted_iota(jnp.int32, (fr, fr), 0)
                    == lax.broadcasted_iota(jnp.int32, (fr, fr), 1), RIDGE, 0.0)
    hot_ref[...] = onehot

    def some_grams(step, carry):
        for j in range(GRAMS):
            mask = hot_ref[pl.ds(step * GRAMS + j, 1), :].astype(BF16)
            left_ref[2 * j * fr:(2 * j + 1) * fr, :] = hi[...] * mask
            left_ref[(2 * j + 1) * fr:(2 * j + 2) * fr, :] = lo[...] * mask
        both = dot_nn(left_ref[...], z_ref[...])
        for j in range(GRAMS):
            gram = both[2 * j * fr:(2 * j + 1) * fr] + both[(2 * j + 1) * fr:(2 * j + 2) * fr]
            at = pl.multiple_of((step * GRAMS + j) * fr, fr)
            put_lanes(mat, pl.ds(at, fr), 0, gram + eye)
        return carry

    lax.fori_loop(0, MEM_DEV // GRAMS, some_grams, 0)
    rm = resid * onehot
    rm_high = rm.astype(BF16)
    rm_low = (rm - rm_high.astype(F32)).astype(BF16)
    rhs = dot_nn(rm_high, z_ref[...]) + dot_nn(rm_low, z_ref[...])

    def panel_rows(k0):
        return [get_lanes(mat, pl.ds(k0 + i, MEM_DEV, stride=fr), (k0 // 128) * 128)
                for i in range(PANEL)]

    ahead = panel_rows(0)
    for k0 in range(0, fr, PANEL):
        lane0 = (k0 // 128) * 128
        orig = ahead
        wide = (MEM_DEV, 128)
        rows = [[o[:, c:c + 128] for c in range(0, o.shape[1], 128)]
                + [jnp.broadcast_to(rhs[:, k0 + i:k0 + i + 1], wide)]
                for i, o in enumerate(orig)]
        reduce_block(rows, k0 - lane0, range(BLOCK), range(BLOCK, PANEL))
        reduce_block(rows, k0 - lane0, range(BLOCK, PANEL), range(BLOCK))
        ys = [jnp.concatenate([r[-1]] * (len(r) - 1), axis=1) for r in rows]
        rows = [r[0] if len(r) == 2 else jnp.concatenate(r[:-1], axis=1) for r in rows]
        tail = rhs[:, lane0:]
        lanes = lax.broadcasted_iota(jnp.int32, tail.shape, 1) + lane0
        drop = jnp.zeros_like(tail)
        place = tail
        for i in range(PANEL):
            drop = drop + orig[i] * ys[i]
            place = jnp.where(lanes == k0 + i, ys[i], place)
        tail = jnp.where(lanes >= k0 + PANEL, tail - drop, place)
        rhs = tail if lane0 == 0 else jnp.concatenate([rhs[:, :lane0], tail], axis=1)
        for i in range(PANEL):
            put_lanes(red, slice((k0 + i) * MEM_DEV, (k0 + i + 1) * MEM_DEV), lane0, rows[i])
        top = k0 + PANEL
        if top < fr:
            lane1 = (top // 128) * 128
            row1 = lane1
            lefts, rights = [], []
            for m in range(MEM_DEV):
                o = get_lanes(mat, pl.ds(m * fr + k0, PANEL), row1)
                w = get_lanes(red, pl.ds(k0 * MEM_DEV + m, PANEL, stride=MEM_DEV), lane1)
                o1, o2, o3 = three_parts(o)
                w1, w2, w3 = three_parts(w)
                left = jnp.concatenate([o1, o1, o2, o2, o1, o3], axis=0)
                lefts.append(left.T[top - row1:])
                rights.append(jnp.concatenate([w1, w2, w1, w2, w3, w1], axis=0))

            def trailing(m, skip, count):
                rest = pl.ds(m * fr + top + skip, count)
                put_lanes(mat, rest, lane1, get_lanes(mat, rest, lane1)
                          - dot_nn(lefts[m][skip:skip + count], rights[m]))

            for m in range(MEM_DEV):
                trailing(m, 0, PANEL)
            ahead = panel_rows(top)
            if top + PANEL < fr:
                for m in range(MEM_DEV):
                    trailing(m, PANEL, fr - top - PANEL)

    lanes = lax.broadcasted_iota(jnp.int32, rhs.shape, 1)
    sol = jnp.where(lanes >= fr - PANEL, rhs, 0.0)
    for k0 in range(fr - 2 * PANEL, -1, -PANEL):
        new = sol
        lane0 = (k0 // 128) * 128
        for i in range(PANEL):
            w = get_lanes(red, slice((k0 + i) * MEM_DEV, (k0 + i + 1) * MEM_DEV), lane0)
            d = jnp.sum(w * sol[:, lane0:], axis=1, keepdims=True)
            new = jnp.where(lanes == k0 + i, rhs - d, new)
        sol = new
    coef = -sol
    coef_ref[...] = coef
    chigh = coef.astype(BF16)
    clow = (coef - chigh.astype(F32)).astype(BF16)
    scores = dot_nn(chigh, zt[...]) + dot_nn(clow, zt[...])
    back = jnp.sum(scores * onehot, axis=0, keepdims=True)
    for o in range(owners):
        back_ref[o] = back[:, o * cap:(o + 1) * cap]


def unpack_kernel(back_ref, slot_ref, out_ref):
    owners, _, cap = back_ref.shape
    back = back_ref[:, 0, :]
    hot_owner, hot_cap = owner_hot(slot_ref[...], owners, cap)
    rows = dot_tn(back, hot_owner, HIGH)
    out_ref[...] = jnp.sum(rows * hot_cap, axis=0, keepdims=True)


VMEM_LIMIT = 32 * 1024 * 1024
STAGE_LIMIT = 20 * 1024 * 1024


def on_chip(kernel, name, outs, *ins, scratch=()):
    vmem = pl.BlockSpec(memory_space=pltpu.VMEM)
    return pl.pallas_call(
        kernel,
        in_specs=[vmem] * len(ins),
        out_specs=[vmem] * len(outs),
        out_shape=[jax.ShapeDtypeStruct(s, d) for s, d in outs],
        scratch_shapes=list(scratch),
        compiler_params=pltpu.CompilerParams(vmem_limit_bytes=STAGE_LIMIT),
        name=name,
    )(*ins)


PH1 = ("core", "z")
PH2 = ("x", "y")


def on_device(features, re_features, member_id, slot, labels, offsets, feature_scale, w_start,
              *, sizes):
    n1 = sizes["core"] * sizes["z"]
    n2 = sizes["x"] * sizes["y"]
    n_mem = sizes["y"] * sizes["z"]
    n_grp = sizes["x"] * sizes["core"]
    rows, f = features.shape
    fr = re_features.shape[1]
    slots = 2 * rows
    cap = slots // n_mem
    def exchange(v, axes):
        return lax.all_to_all(v, axes, 0, 0, tiled=True)

    def reduce_rest(parts):
        got = exchange(parts, PH1)
        mid, = on_chip(again_kernel, "again", [((n2, 1, f), F32)], got)
        return exchange(mid, PH2)

    def reduce_permutes(v):
        half = sizes["z"] // 2
        four = (1, 2, 3)
        for axis, flips in (("x", four), ("core", (1,)), ("y", four), ("z", four), ("z", (half,))):
            size = sizes[axis]
            moved = [lax.ppermute(v, axis, [(i, i ^ b) for i in range(size)]) for b in flips]
            v, = on_chip(add_kernel, "add", [((1, 1, f), F32)], v, *moved)
        return v

    tmp = [pltpu.VMEM((8, f), BF16), pltpu.VMEM((8, rows), BF16)]
    vec = ((1, f), F32)
    small = ((1, 128), F32)
    row = ((1, rows), F32)
    parts = ((n1, 1, f), F32)
    vmem = pl.BlockSpec(memory_space=pltpu.VMEM)
    hbm = pl.BlockSpec(memory_space=pltpu.HBM)
    outs = [((1, rows), jnp.int32), row, row, row, vec, vec,
            ((1, 1, f), F32), row, row]
    packed, slot_row, code, lab, off, scale, w, gpart, score, curv = pl.pallas_call(
        start_kernel,
        in_specs=[hbm] * 8,
        out_specs=[hbm] + [vmem] * len(outs),
        out_shape=[pltpu.HBM((slots, fr), BF16)] + [jax.ShapeDtypeStruct(*o) for o in outs],
        scratch_shapes=[pltpu.VMEM((rows, f), BF16), pltpu.VMEM((rows, fr), BF16)] + [pltpu.VMEM((1, rows), jnp.int32)] * 2
        + [pltpu.VMEM((8, slots // 8, fr), BF16)] + tmp
        + [pltpu.SemaphoreType.DMA((7,)), pltpu.SemaphoreType.DMA((STEPS,)),
           pltpu.SemaphoreType.DMA((8,))],
        compiler_params=pltpu.CompilerParams(vmem_limit_bytes=STAGE_LIMIT),
        name="start",
    )(*[pltpu.with_memory_space_constraint(v, pltpu.HBM) for v in (
        features, re_features, slot.reshape(1, rows), member_id.reshape(1, rows),
        labels.reshape(1, rows), offsets.reshape(1, rows), feature_scale.reshape(1, f),
        w_start.reshape(1, f))])
    z_got = lax.all_to_all(packed.reshape(n_mem, cap, fr), ("y", "z"), 0, 0, tiled=True)
    z_got = z_got.reshape(slots, fr)
    for it in range(NEWTON):
        if it == 0:
            g2, z_got = lax.optimization_barrier((reduce_permutes(gpart), z_got))
        else:
            g2 = reduce_rest(gpart)
        if it == 0:
            x, hpart, p, rr, t = pl.pallas_call(
                cg_load_kernel,
                in_specs=[hbm] + [vmem] * 4,
                out_specs=[vmem] * 5,
                out_shape=[jax.ShapeDtypeStruct((rows, f), BF16)]
                + [jax.ShapeDtypeStruct(*o) for o in (parts, vec, small, row)],
                scratch_shapes=tmp + [pltpu.SemaphoreType.DMA((STEPS,))],
                compiler_params=pltpu.CompilerParams(vmem_limit_bytes=STAGE_LIMIT),
                name="cg_load",
            )(pltpu.with_memory_space_constraint(features, pltpu.HBM), g2, scale, w, curv)
        else:
            hpart, p, rr, t = on_chip(cg_first_kernel, "cg_first", [parts, vec, small, row],
                                      x, g2, scale, w, curv, scratch=tmp)
        h2 = reduce_rest(hpart)
        hpart, p, r, u, rr, t, m = on_chip(
            cg_next_kernel, "cg_next", [parts, vec, vec, vec, small, row, row],
            x, h2, scale, curv, p, rr, t, scratch=tmp)
        h2 = reduce_rest(hpart)
        ins = (x, h2, scale, curv, p, r, u, rr, t, m)
        if it + 1 < NEWTON:
            spart, p, u, rr, t, m = on_chip(
                cg_last_kernel, "cg_last", [((n1 * n2, 1, 128), F32), vec, vec, small, row, row],
                *ins, scratch=tmp)
            sgot = exchange(spart, ("x", "core", "y", "z"))
            gpart, w, score, curv = on_chip(
                grad_next_kernel, "grad_next", [parts, vec, row, row],
                x, sgot, rr, w, u, p, score, t, m, off, lab, scratch=tmp)
        else:
            send, p, u, rr = on_chip(
                cg_last_pack_kernel, "cg_last_pack",
                [((n_mem, 1, 4 * cap), F32), vec, vec, small],
                *ins, score, slot_row, code, scratch=[pltpu.VMEM((1, rows), F32)] + tmp)
    got = exchange(send, ("y", "z"))
    part, = on_chip(part_kernel, "part", [((n_grp, 1, 128), F32)], got)
    part = exchange(part, ("x", "core"))
    z_got = pltpu.with_memory_space_constraint(z_got, pltpu.HBM)
    w, member_coef, back = pl.pallas_call(
        member_kernel,
        in_specs=[pl.BlockSpec(memory_space=pltpu.HBM)] + [vmem] * 6,
        out_shape=[jax.ShapeDtypeStruct((1, f), F32),
                   jax.ShapeDtypeStruct((MEM_DEV, fr), F32),
                   jax.ShapeDtypeStruct((n_mem, 1, cap), F32)],
        scratch_shapes=[pltpu.VMEM((1, slots), F32)] * 3
        + [pltpu.VMEM((fr, slots), BF16)] * 3
        + [pltpu.VMEM((MEM_DEV * fr, 128), F32)] * 4
        + [pltpu.VMEM((slots, fr), BF16), pltpu.VMEM((MEM_DEV, slots), F32),
           pltpu.VMEM((2 * GRAMS * fr, slots), BF16),
           pltpu.SemaphoreType.DMA(())],
        compiler_params=pltpu.CompilerParams(vmem_limit_bytes=VMEM_LIMIT),
        name="members",
    )(z_got, got, part, rr, w, u, p)
    returned = exchange(back, ("y", "z"))
    row_offsets = pl.pallas_call(
        unpack_kernel,
        out_shape=jax.ShapeDtypeStruct((1, rows), F32),
        compiler_params=pltpu.CompilerParams(vmem_limit_bytes=VMEM_LIMIT),
        name="unpack",
    )(returned, slot_row)
    return (w.reshape(f), member_coef, row_offsets.reshape(rows))


def solution(mesh):
    n_grp, n_mem = mesh.shape["grp"], mesh.shape["mem"]
    shape = {"x": n_grp // 2, "core": 2, "y": 4, "z": n_mem // 4}
    fine = Mesh(mesh.devices.reshape(tuple(shape.values())), tuple(shape))
    cut = P(("x", "core", "y", "z"))
    cut2 = P(("x", "core", "y", "z"), None)
    return jax.shard_map(
        functools.partial(on_device, sizes=shape),
        mesh=fine,
        in_specs=(cut2, cut2, cut, cut, cut, cut, P(), P()),
        out_specs=(P(), cut2, cut),
        check_vma=False,
    )
```

```python
import functools
import jax
import jax.numpy as jnp
from jax import lax
from jax.experimental import pallas as pl
from jax.experimental.pallas import tpu as pltpu
from jax.sharding import Mesh, PartitionSpec as P

MEM_DEV = 8
NEWTON = 2
RIDGE = 1.0
PANEL = 16
BLOCK = 8
STEPS = 4
F_STEPS = 2
B_STEPS = 2
GRAMS = 2
F32 = jnp.float32
BF16 = jnp.bfloat16
HIGH = lax.Precision.HIGHEST


def dot_nn(a, b, precision=None):
    return lax.dot_general(a, b, (((1,), (0,)), ((), ())), precision=precision,
                           preferred_element_type=F32)


def dot_nt(a, b, precision=None):
    return lax.dot_general(a, b, (((1,), (1,)), ((), ())), precision=precision,
                           preferred_element_type=F32)


def dot_tn(a, b, precision=None):
    return lax.dot_general(a, b, (((0,), (0,)), ((), ())), precision=precision,
                           preferred_element_type=F32)


def split_rows(row):
    high = row.astype(BF16).astype(F32)
    low = row - high
    at = lax.broadcasted_iota(jnp.int32, (8, row.shape[1]), 0)
    return jnp.where(at == 0, high, jnp.where(at == 1, low, 0.0)).astype(BF16)


def sigmoid(x):
    return 1.0 / (1.0 + jnp.exp(-x))


def total(row):
    return jnp.sum(row, axis=1, keepdims=True)


def sum_parts(ref):
    acc = ref[0]
    for i in range(1, ref.shape[0]):
        acc = acc + ref[i]
    return acc


def forward(xs, x_ref, xs_ref, row_ref, arrive=None, steps=STEPS):
    xs_ref[...] = xs
    block = x_ref.shape[0] // steps

    def body(i, carry):
        at = pl.multiple_of(i * block, block)
        if arrive is not None:
            arrive(i, at, block)
        both = dot_nt(xs_ref[...], x_ref[pl.ds(at, block), :])
        row_ref[:, pl.ds(at, block)] = both[0:1] + both[1:2]
        return carry

    lax.fori_loop(0, steps, body, 0)
    return row_ref[...]


def backward(row, x_ref, split_ref, out_ref):
    split_ref[...] = split_rows(row)
    block = x_ref.shape[1] // B_STEPS

    def body(i, carry):
        at = pl.multiple_of(i * block, block)
        both = dot_nn(split_ref[...], x_ref[:, pl.ds(at, block)])
        val = both[0:1] + both[1:2]
        for j in range(out_ref.shape[0]):
            out_ref[j, :, pl.ds(at, block)] = val
        return carry

    lax.fori_loop(0, B_STEPS, body, 0)


def start_kernel(x_hbm, z_hbm, slot_hbm, member_hbm, lab_hbm, off_hbm, scale_hbm, w_hbm,
                 packed_ref, slot_ref, code_ref, lab_ref, off_ref, scale_ref, w_ref,
                 out_ref, score_ref, curv_ref,
                 x_ref, z_ref, member_ref, int_ref, buf, xs_ref, split_ref, sems, xsems, psems):
    pairs = [(slot_hbm, slot_ref), (z_hbm, z_ref), (scale_hbm, scale_ref), (w_hbm, w_ref),
             (member_hbm, member_ref), (lab_hbm, int_ref), (off_hbm, off_ref)]
    loads = [pltpu.make_async_copy(src, dst, sems.at[i]) for i, (src, dst) in enumerate(pairs)]
    for load in loads:
        load.start()

    def chunk(i, at, block):
        return pltpu.make_async_copy(x_hbm.at[pl.ds(at, block)], x_ref.at[pl.ds(at, block)],
                                     xsems.at[i])

    block = x_ref.shape[0] // STEPS
    for i in range(STEPS):
        chunk(i, i * block, block).start()
    loads[0].wait()
    loads[1].wait()
    size = buf.shape[1]

    def store(b):
        at = b * size if isinstance(b, int) else pl.multiple_of(b * size, size)
        return pltpu.make_async_copy(buf.at[b], packed_ref.at[pl.ds(at, size)], psems.at[b])

    def pack(b, carry):
        rows = lax.broadcasted_iota(jnp.int32, (size, slot_ref.shape[1]), 0) + b * size
        hot = jnp.where(rows == slot_ref[...], 1.0, 0.0).astype(BF16)
        buf[b] = dot_nn(hot, z_ref[...]).astype(BF16)
        store(b).start()
        return carry

    lax.fori_loop(0, buf.shape[0], pack, 0)
    for load in loads[2:]:
        load.wait()
    labels = int_ref[...]
    lab_ref[...] = labels.astype(F32)
    code_ref[...] = (member_ref[...] % MEM_DEV + 8 * labels + 16).astype(F32)
    score = forward(split_rows(scale_ref[...] * w_ref[...]), x_ref, xs_ref, score_ref,
                    lambda i, at, size: chunk(i, at, size).wait())
    prob = sigmoid(score + off_ref[...])
    curv_ref[...] = prob * (1.0 - prob)
    backward(prob - lab_ref[...], x_ref, split_ref, out_ref)
    for b in range(buf.shape[0]):
        store(b).wait()


def grad_next_kernel(x_ref, part_ref, rr_ref, w_ref, u_ref, p_ref, score_ref, t_ref, m_ref,
                     off_ref, lab_ref, out_ref, w_out, score_out, curv_ref, xs_ref, split_ref):
    a = last_coef(part_ref, rr_ref, p_ref)
    w_out[...] = w_ref[...] + (u_ref[...] + a * p_ref[...])
    score = score_ref[...] + (m_ref[...] + a * t_ref[...])
    prob = sigmoid(score + off_ref[...])
    score_out[...] = score
    curv_ref[...] = prob * (1.0 - prob)
    backward(prob - lab_ref[...], x_ref, split_ref, out_ref)


def last_coef(part_ref, rr_ref, p_ref):
    p = p_ref[...]
    php = jnp.sum(part_ref[:, 0, :], axis=0, keepdims=True)[:, 0:1] + RIDGE * total(p * p)
    return rr_ref[:, 0:1] / php


def cg_first_kernel(x_ref, sum_ref, scale_ref, w_ref, curv_ref, out_ref, p_out, rr_out, t_ref,
                    xs_ref, split_ref, arrive=None):
    r = -(scale_ref[...] * sum_parts(sum_ref) + RIDGE * w_ref[...])
    p_out[...] = r
    rr_out[...] = jnp.broadcast_to(total(r * r), rr_out.shape)
    t = forward(split_rows(scale_ref[...] * r), x_ref, xs_ref, t_ref, arrive,
                STEPS if arrive else F_STEPS)
    backward(curv_ref[...] * t, x_ref, split_ref, out_ref)


def cg_load_kernel(x_hbm, sum_ref, scale_ref, w_ref, curv_ref, x_ref, out_ref, p_out, rr_out,
                   t_ref, xs_ref, split_ref, sems):
    def chunk(i, at, block):
        return pltpu.make_async_copy(x_hbm.at[pl.ds(at, block)], x_ref.at[pl.ds(at, block)],
                                     sems.at[i])

    block = x_ref.shape[0] // STEPS
    for i in range(STEPS):
        chunk(i, i * block, block).start()
    cg_first_kernel(x_ref, sum_ref, scale_ref, w_ref, curv_ref, out_ref, p_out, rr_out, t_ref,
                    xs_ref, split_ref, lambda i, at, size: chunk(i, at, size).wait())


def cg_update(sum_ref, scale_ref, p_ref, r_ref, u_ref, rr_ref, p_out, r_out, u_out, rr_out):
    p = p_ref[...]
    q = scale_ref[...] * sum_parts(sum_ref) + RIDGE * p
    rr = rr_ref[:, 0:1]
    a = rr / total(p * q)
    u = a * p if u_ref is None else u_ref[...] + a * p
    r = r_ref[...] - a * q
    nn = total(r * r)
    p = r + (nn / rr) * p
    u_out[...] = u
    if r_out is not None:
        r_out[...] = r
    p_out[...] = p
    rr_out[...] = jnp.broadcast_to(nn, rr_out.shape)
    return a, split_rows(scale_ref[...] * p)


def cg_next_kernel(x_ref, sum_ref, scale_ref, curv_ref, p_ref, rr_ref, t_in,
                   out_ref, p_out, r_out, u_out, rr_out, t_ref, m_ref, xs_ref, split_ref):
    a, xs = cg_update(sum_ref, scale_ref, p_ref, p_ref, None, rr_ref, p_out, r_out, u_out, rr_out)
    m_ref[...] = a * t_in[...]
    t = forward(xs, x_ref, xs_ref, t_ref, steps=F_STEPS)
    backward(curv_ref[...] * t, x_ref, split_ref, out_ref)


def cg_last_kernel(x_ref, sum_ref, scale_ref, curv_ref, p_ref, r_ref, u_ref, rr_ref, t_in, m_in,
                   out_ref, p_out, u_out, rr_out, t_ref, m_ref, xs_ref, split_ref):
    a, xs = cg_update(sum_ref, scale_ref, p_ref, r_ref, u_ref, rr_ref, p_out, None, u_out, rr_out)
    m_ref[...] = m_in[...] + a * t_in[...]
    t = forward(xs, x_ref, xs_ref, t_ref)
    out_ref[...] = jnp.broadcast_to(total(curv_ref[...] * t * t).reshape(1, 1, 1), out_ref.shape)


def owner_hot(slot, owners, cap):
    rows = lax.broadcasted_iota(jnp.int32, (owners, slot.shape[1]), 0)
    hot_owner = jnp.where(rows == slot // cap, 1.0, 0.0)
    lanes = lax.broadcasted_iota(jnp.int32, (cap, slot.shape[1]), 0)
    hot_cap = jnp.where(lanes == slot % cap, 1.0, 0.0)
    return hot_owner, hot_cap


def cg_last_pack_kernel(x_ref, sum_ref, scale_ref, curv_ref, p_ref, r_ref, u_ref, rr_ref, t_in,
                        m_in, score_ref, slot_ref, code_ref, out_ref, p_out, u_out, rr_out,
                        t_ref, xs_ref, split_ref):
    a, xs = cg_update(sum_ref, scale_ref, p_ref, r_ref, u_ref, rr_ref, p_out, None, u_out, rr_out)
    owners, cap = out_ref.shape[0], out_ref.shape[2] // 4
    hot_owner, hot_cap = owner_hot(slot_ref[...], owners, cap)
    t = forward(xs, x_ref, xs_ref, t_ref)
    done = score_ref[...] + (m_in[...] + a * t_in[...])
    php = total(curv_ref[...] * t * t)
    left = jnp.concatenate([hot_owner * done, hot_owner * t, hot_owner * code_ref[...]], axis=0)
    send = dot_nt(left, hot_cap, HIGH)
    part = jnp.broadcast_to(php, (1, cap))
    for i in range(owners):
        out_ref[i] = jnp.concatenate(
            [send[j * owners + i:j * owners + i + 1] for j in range(3)] + [part], axis=1)


def again_kernel(sum_ref, out_ref):
    val = sum_parts(sum_ref)
    for i in range(out_ref.shape[0]):
        out_ref[i] = val


def add_kernel(*refs):
    out_ref = refs[-1]
    vals = [ref[...] for ref in refs[:-1]]
    while len(vals) > 1:
        vals = [vals[i] + vals[i + 1] for i in range(0, len(vals), 2)]
    out_ref[...] = vals[0]


def part_kernel(arr_ref, out_ref):
    last = arr_ref.shape[2] - 1
    got = arr_ref[:, 0, :]
    val = jnp.sum(got, axis=0, keepdims=True)[:, last:]
    out_ref[...] = jnp.broadcast_to(val.reshape(1, 1, 1), out_ref.shape)


def three_parts(v):
    a = v.astype(BF16)
    rest = v - a.astype(F32)
    b = rest.astype(BF16)
    c = (rest - b.astype(F32)).astype(BF16)
    return a, b, c


def get_lanes(halves, rows, lane):
    if lane:
        return halves[1][rows, :]
    return jnp.concatenate([halves[0][rows, :], halves[1][rows, :]], axis=1)


def put_lanes(halves, rows, lane, value):
    if lane:
        halves[1][rows, :] = value
    else:
        halves[0][rows, :] = value[:, :128]
        halves[1][rows, :] = value[:, 128:]


def reduce_block(rows, lane, block, others):
    def at(i, j):
        return jnp.broadcast_to(rows[i][0][:, lane + j:lane + j + 1], rows[i][0].shape)

    block, others = list(block), list(others)
    c = {(i, j): at(i, j) for i in block for j in block if j <= i}
    far = {(i, j): at(i, j) for i in others for j in block}
    lower, inv = {}, {}
    for j in block:
        inv[j] = 1.0 / c[j, j]
        for i in block:
            if i > j:
                lower[i, j] = c[i, j] * inv[j]
        for i in block:
            for k in block:
                if j < k <= i:
                    c[i, k] = c[i, k] - lower[i, j] * c[k, j]
    for j in block:
        for i in block:
            if i > j:
                rows[i] = [v - lower[i, j] * w for v, w in zip(rows[i], rows[j])]
    for j in block:
        rows[j] = [w * inv[j] for w in rows[j]]
    for j in reversed(block):
        for i in block:
            if i < j:
                rows[i] = [v - lower[j, i] * w for v, w in zip(rows[i], rows[j])]
    for j in block:
        for i in others:
            rows[i] = [v - far[i, j] * w for v, w in zip(rows[i], rows[j])]


def member_kernel(z_hbm, arr_ref, part_ref, rr_ref, w_ref, u_ref, p_ref,
                  w_out, coef_ref, back_ref,
                  base, tvec, code, zt, hi, lo, mat0, mat1, red0, red1, z_ref, hot_ref,
                  left_ref, sem):
    copy = pltpu.make_async_copy(z_hbm, z_ref, sem)
    copy.start()
    owners = arr_ref.shape[0]
    cap = arr_ref.shape[2] // 4
    fr = z_ref.shape[1]
    slots = z_ref.shape[0]
    p = p_ref[...]
    php = jnp.sum(part_ref[:, 0, :], axis=0, keepdims=True)[:, 0:1] + RIDGE * total(p * p)
    a = rr_ref[:, 0:1] / php
    w_out[...] = w_ref[...] + (u_ref[...] + a * p)
    for o in range(owners):
        got = arr_ref[o]
        base[:, o * cap:(o + 1) * cap] = got[:, 0:cap]
        tvec[:, o * cap:(o + 1) * cap] = got[:, cap:2 * cap]
        code[:, o * cap:(o + 1) * cap] = got[:, 2 * cap:3 * cap]
    prob = sigmoid(base[...] + a * tvec[...])
    curv = prob * (1.0 - prob)
    codes = code[...]
    label = jnp.where(codes >= 24.0, 1.0, 0.0)
    resid = prob - label
    local = codes - 16.0 - 8.0 * label
    at = lax.broadcasted_iota(jnp.int32, (MEM_DEV, slots), 0).astype(F32)
    onehot = jnp.where(local == at, 1.0, 0.0)

    copy.wait()
    z_t = z_ref[...].T
    zt[...] = z_t
    chunk = 512
    for c in range(0, slots, chunk):
        cz = zt[:, c:c + chunk].astype(F32) * curv[:, c:c + chunk]
        high = cz.astype(BF16)
        hi[:, c:c + chunk] = high
        lo[:, c:c + chunk] = (cz - high.astype(F32)).astype(BF16)
    mat, red = (mat0, mat1), (red0, red1)
    eye = jnp.where(lax.broadcasted_iota(jnp.int32, (fr, fr), 0)
                    == lax.broadcasted_iota(jnp.int32, (fr, fr), 1), RIDGE, 0.0)
    hot_ref[...] = onehot

    def some_grams(step, carry):
        for j in range(GRAMS):
            mask = hot_ref[pl.ds(step * GRAMS + j, 1), :].astype(BF16)
            left_ref[2 * j * fr:(2 * j + 1) * fr, :] = hi[...] * mask
            left_ref[(2 * j + 1) * fr:(2 * j + 2) * fr, :] = lo[...] * mask
        both = dot_nn(left_ref[...], z_ref[...])
        for j in range(GRAMS):
            gram = both[2 * j * fr:(2 * j + 1) * fr] + both[(2 * j + 1) * fr:(2 * j + 2) * fr]
            at = pl.multiple_of((step * GRAMS + j) * fr, fr)
            put_lanes(mat, pl.ds(at, fr), 0, gram + eye)
        return carry

    lax.fori_loop(0, MEM_DEV // GRAMS, some_grams, 0)
    rm = resid * onehot
    rm_high = rm.astype(BF16)
    rm_low = (rm - rm_high.astype(F32)).astype(BF16)
    rhs = dot_nn(rm_high, z_ref[...]) + dot_nn(rm_low, z_ref[...])

    def panel_rows(k0):
        return [get_lanes(mat, pl.ds(k0 + i, MEM_DEV, stride=fr), (k0 // 128) * 128)
                for i in range(PANEL)]

    ahead = panel_rows(0)
    for k0 in range(0, fr, PANEL):
        lane0 = (k0 // 128) * 128
        orig = ahead
        wide = (MEM_DEV, 128)
        rows = [[o[:, c:c + 128] for c in range(0, o.shape[1], 128)]
                + [jnp.broadcast_to(rhs[:, k0 + i:k0 + i + 1], wide)]
                for i, o in enumerate(orig)]
        reduce_block(rows, k0 - lane0, range(BLOCK), range(BLOCK, PANEL))
        reduce_block(rows, k0 - lane0, range(BLOCK, PANEL), range(BLOCK))
        ys = [jnp.concatenate([r[-1]] * (len(r) - 1), axis=1) for r in rows]
        rows = [r[0] if len(r) == 2 else jnp.concatenate(r[:-1], axis=1) for r in rows]
        tail = rhs[:, lane0:]
        lanes = lax.broadcasted_iota(jnp.int32, tail.shape, 1) + lane0
        drop = jnp.zeros_like(tail)
        place = tail
        for i in range(PANEL):
            drop = drop + orig[i] * ys[i]
            place = jnp.where(lanes == k0 + i, ys[i], place)
        tail = jnp.where(lanes >= k0 + PANEL, tail - drop, place)
        rhs = tail if lane0 == 0 else jnp.concatenate([rhs[:, :lane0], tail], axis=1)
        for i in range(PANEL):
            put_lanes(red, slice((k0 + i) * MEM_DEV, (k0 + i + 1) * MEM_DEV), lane0, rows[i])
        top = k0 + PANEL
        if top < fr:
            lane1 = (top // 128) * 128
            row1 = lane1
            lefts, rights = [], []
            for m in range(MEM_DEV):
                o = get_lanes(mat, pl.ds(m * fr + k0, PANEL), row1)
                w = get_lanes(red, pl.ds(k0 * MEM_DEV + m, PANEL, stride=MEM_DEV), lane1)
                o1, o2, o3 = three_parts(o)
                w1, w2, w3 = three_parts(w)
                left = jnp.concatenate([o1, o1, o2, o2, o1, o3], axis=0)
                lefts.append(left.T[top - row1:])
                rights.append(jnp.concatenate([w1, w2, w1, w2, w3, w1], axis=0))

            def trailing(m, skip, count):
                rest = pl.ds(m * fr + top + skip, count)
                put_lanes(mat, rest, lane1, get_lanes(mat, rest, lane1)
                          - dot_nn(lefts[m][skip:skip + count], rights[m]))

            for m in range(MEM_DEV):
                trailing(m, 0, PANEL)
            ahead = panel_rows(top)
            if top + PANEL < fr:
                for m in range(MEM_DEV):
                    trailing(m, PANEL, fr - top - PANEL)

    lanes = lax.broadcasted_iota(jnp.int32, rhs.shape, 1)
    sol = jnp.where(lanes >= fr - PANEL, rhs, 0.0)
    for k0 in range(fr - 2 * PANEL, -1, -PANEL):
        new = sol
        lane0 = (k0 // 128) * 128
        for i in range(PANEL):
            w = get_lanes(red, slice((k0 + i) * MEM_DEV, (k0 + i + 1) * MEM_DEV), lane0)
            d = jnp.sum(w * sol[:, lane0:], axis=1, keepdims=True)
            new = jnp.where(lanes == k0 + i, rhs - d, new)
        sol = new
    coef = -sol
    coef_ref[...] = coef
    chigh = coef.astype(BF16)
    clow = (coef - chigh.astype(F32)).astype(BF16)
    scores = dot_nn(chigh, zt[...]) + dot_nn(clow, zt[...])
    back = jnp.sum(scores * onehot, axis=0, keepdims=True)
    for o in range(owners):
        back_ref[o] = back[:, o * cap:(o + 1) * cap]


def unpack_kernel(back_ref, slot_ref, out_ref):
    owners, _, cap = back_ref.shape
    back = back_ref[:, 0, :]
    hot_owner, hot_cap = owner_hot(slot_ref[...], owners, cap)
    rows = dot_tn(back, hot_owner, HIGH)
    out_ref[...] = jnp.sum(rows * hot_cap, axis=0, keepdims=True)


VMEM_LIMIT = 32 * 1024 * 1024
STAGE_LIMIT = 20 * 1024 * 1024


def on_chip(kernel, name, outs, *ins, scratch=()):
    vmem = pl.BlockSpec(memory_space=pltpu.VMEM)
    return pl.pallas_call(
        kernel,
        in_specs=[vmem] * len(ins),
        out_specs=[vmem] * len(outs),
        out_shape=[jax.ShapeDtypeStruct(s, d) for s, d in outs],
        scratch_shapes=list(scratch),
        compiler_params=pltpu.CompilerParams(vmem_limit_bytes=STAGE_LIMIT),
        name=name,
    )(*ins)


PH1 = ("x", "y")
PH2 = ("core", "z")


def on_device(features, re_features, member_id, slot, labels, offsets, feature_scale, w_start,
              *, sizes):
    n1 = sizes["x"] * sizes["y"]
    n2 = sizes["core"] * sizes["z"]
    n_mem = sizes["y"] * sizes["z"]
    n_grp = sizes["x"] * sizes["core"]
    rows, f = features.shape
    fr = re_features.shape[1]
    slots = 2 * rows
    cap = slots // n_mem
    def exchange(v, axes):
        return lax.all_to_all(v, axes, 0, 0, tiled=True)

    def reduce_rest(parts):
        got = exchange(parts, PH1)
        mid, = on_chip(again_kernel, "again", [((n2, 1, f), F32)], got)
        return exchange(mid, PH2)

    def reduce_permutes(v):
        half = sizes["z"] // 2
        four = (1, 2, 3)
        for axis, flips in (("x", four), ("core", (1,)), ("y", four), ("z", four), ("z", (half,))):
            size = sizes[axis]
            moved = [lax.ppermute(v, axis, [(i, i ^ b) for i in range(size)]) for b in flips]
            v, = on_chip(add_kernel, "add", [((1, 1, f), F32)], v, *moved)
        return v

    tmp = [pltpu.VMEM((8, f), BF16), pltpu.VMEM((8, rows), BF16)]
    vec = ((1, f), F32)
    small = ((1, 128), F32)
    row = ((1, rows), F32)
    parts = ((n1, 1, f), F32)
    vmem = pl.BlockSpec(memory_space=pltpu.VMEM)
    hbm = pl.BlockSpec(memory_space=pltpu.HBM)
    outs = [((1, rows), jnp.int32), row, row, row, vec, vec,
            ((1, 1, f), F32), row, row]
    packed, slot_row, code, lab, off, scale, w, gpart, score, curv = pl.pallas_call(
        start_kernel,
        in_specs=[hbm] * 8,
        out_specs=[hbm] + [vmem] * len(outs),
        out_shape=[pltpu.HBM((slots, fr), BF16)] + [jax.ShapeDtypeStruct(*o) for o in outs],
        scratch_shapes=[pltpu.VMEM((rows, f), BF16), pltpu.VMEM((rows, fr), BF16)] + [pltpu.VMEM((1, rows), jnp.int32)] * 2
        + [pltpu.VMEM((8, slots // 8, fr), BF16)] + tmp
        + [pltpu.SemaphoreType.DMA((7,)), pltpu.SemaphoreType.DMA((STEPS,)),
           pltpu.SemaphoreType.DMA((8,))],
        compiler_params=pltpu.CompilerParams(vmem_limit_bytes=STAGE_LIMIT),
        name="start",
    )(*[pltpu.with_memory_space_constraint(v, pltpu.HBM) for v in (
        features, re_features, slot.reshape(1, rows), member_id.reshape(1, rows),
        labels.reshape(1, rows), offsets.reshape(1, rows), feature_scale.reshape(1, f),
        w_start.reshape(1, f))])
    z_got = lax.all_to_all(packed.reshape(n_mem, cap, fr), ("y", "z"), 0, 0, tiled=True)
    z_got = z_got.reshape(slots, fr)
    for it in range(NEWTON):
        if it == 0:
            g2, z_got = lax.optimization_barrier((reduce_permutes(gpart), z_got))
        else:
            g2 = reduce_rest(gpart)
        if it == 0:
            x, hpart, p, rr, t = pl.pallas_call(
                cg_load_kernel,
                in_specs=[hbm] + [vmem] * 4,
                out_specs=[vmem] * 5,
                out_shape=[jax.ShapeDtypeStruct((rows, f), BF16)]
                + [jax.ShapeDtypeStruct(*o) for o in (parts, vec, small, row)],
                scratch_shapes=tmp + [pltpu.SemaphoreType.DMA((STEPS,))],
                compiler_params=pltpu.CompilerParams(vmem_limit_bytes=STAGE_LIMIT),
                name="cg_load",
            )(pltpu.with_memory_space_constraint(features, pltpu.HBM), g2, scale, w, curv)
        else:
            hpart, p, rr, t = on_chip(cg_first_kernel, "cg_first", [parts, vec, small, row],
                                      x, g2, scale, w, curv, scratch=tmp)
        h2 = reduce_rest(hpart)
        hpart, p, r, u, rr, t, m = on_chip(
            cg_next_kernel, "cg_next", [parts, vec, vec, vec, small, row, row],
            x, h2, scale, curv, p, rr, t, scratch=tmp)
        h2 = reduce_rest(hpart)
        ins = (x, h2, scale, curv, p, r, u, rr, t, m)
        if it + 1 < NEWTON:
            spart, p, u, rr, t, m = on_chip(
                cg_last_kernel, "cg_last", [((n1 * n2, 1, 128), F32), vec, vec, small, row, row],
                *ins, scratch=tmp)
            sgot = exchange(spart, ("x", "core", "y", "z"))
            gpart, w, score, curv = on_chip(
                grad_next_kernel, "grad_next", [parts, vec, row, row],
                x, sgot, rr, w, u, p, score, t, m, off, lab, scratch=tmp)
        else:
            send, p, u, rr = on_chip(
                cg_last_pack_kernel, "cg_last_pack",
                [((n_mem, 1, 4 * cap), F32), vec, vec, small],
                *ins, score, slot_row, code, scratch=[pltpu.VMEM((1, rows), F32)] + tmp)
    got = exchange(send, ("y", "z"))
    part, = on_chip(part_kernel, "part", [((n_grp, 1, 128), F32)], got)
    part = exchange(part, ("x", "core"))
    z_got = pltpu.with_memory_space_constraint(z_got, pltpu.HBM)
    w, member_coef, back = pl.pallas_call(
        member_kernel,
        in_specs=[pl.BlockSpec(memory_space=pltpu.HBM)] + [vmem] * 6,
        out_shape=[jax.ShapeDtypeStruct((1, f), F32),
                   jax.ShapeDtypeStruct((MEM_DEV, fr), F32),
                   jax.ShapeDtypeStruct((n_mem, 1, cap), F32)],
        scratch_shapes=[pltpu.VMEM((1, slots), F32)] * 3
        + [pltpu.VMEM((fr, slots), BF16)] * 3
        + [pltpu.VMEM((MEM_DEV * fr, 128), F32)] * 4
        + [pltpu.VMEM((slots, fr), BF16), pltpu.VMEM((MEM_DEV, slots), F32),
           pltpu.VMEM((2 * GRAMS * fr, slots), BF16),
           pltpu.SemaphoreType.DMA(())],
        compiler_params=pltpu.CompilerParams(vmem_limit_bytes=VMEM_LIMIT),
        name="members",
    )(z_got, got, part, rr, w, u, p)
    returned = exchange(back, ("y", "z"))
    row_offsets = pl.pallas_call(
        unpack_kernel,
        out_shape=jax.ShapeDtypeStruct((1, rows), F32),
        compiler_params=pltpu.CompilerParams(vmem_limit_bytes=VMEM_LIMIT),
        name="unpack",
    )(returned, slot_row)
    return (w.reshape(f), member_coef, row_offsets.reshape(rows))


def solution(mesh):
    n_grp, n_mem = mesh.shape["grp"], mesh.shape["mem"]
    shape = {"x": n_grp // 2, "core": 2, "y": 4, "z": n_mem // 4}
    fine = Mesh(mesh.devices.reshape(tuple(shape.values())), tuple(shape))
    cut = P(("x", "core", "y", "z"))
    cut2 = P(("x", "core", "y", "z"), None)
    return jax.shard_map(
        functools.partial(on_device, sizes=shape),
        mesh=fine,
        in_specs=(cut2, cut2, cut, cut, cut, cut, P(), P()),
        out_specs=(P(), cut2, cut),
        check_vma=False,
    )
```
